32 devices in a mesh: gx: 2 (over x), gy: 8 (over z, y), cp: 2 (over core).
Axes of the slice: x: 2, y: 2, z: 4, core: 2. Of those that a mesh axis runs over, the one named last changes fastest.
Arguments:
- start_vectors: float32 [8, 8, 192, 256], P(None, None, 'gy', 'gx'), may hold values from -6 to 6
- potential: float32 [8, 192, 256], P(None, 'gy', 'gx'), may hold values from -1.1 to 1.1
Outputs:
- filtered_basis: float32 [8, 8, 192, 256], P(None, None, 'gy', 'gx')
- projected: float32 [8, 8], replicated
The draws below stay inside these ranges and needn't reach their ends.
All inputs are finite; a program needn't handle non-finite values.
Results may differ from the reference program's by a relative error of at most 0.0003.
Values sent between devices are 32-bit elements; how exact they have to be, the bound alone decides.
No kernel may reach another device: no remote copies, remote signals or barrier semaphores. Data moves between devices by JAX's collectives and lax.ppermute only.
A program may use at most 64 MiB of HBM per device.

```python
import math
import jax
import jax.numpy as jnp
from jax import lax

M = 8
NZ = 8
POINTS = 4
ITERS = 3
NX = 256
NY = 192


def draw_potential(key, part):
    phase_key, rough_key = jax.random.split(jax.random.fold_in(key, 11))
    phase = jax.random.uniform(phase_key, (), jnp.float32, 0.0, 2.0 * math.pi)
    rows = jnp.arange(NY, dtype=jnp.float32)[None, :, None]
    smooth = 0.6
    rough = 0.5
    noise = jax.random.uniform(rough_key, (NZ, NY, NX), jnp.float32, -1.0, 1.0)
    return smooth * jnp.cos(2.0 * math.pi * rows / NY + phase) + rough * noise


def shard_levels(rng, shape, pieces, smallest, top_value):
    gain, own = 1.0, jax.random.fold_in(rng, 6)
    for position, parts in pieces:
        steps = jnp.exp(jax.random.uniform(jax.random.fold_in(own, position), (parts,), jnp.float32, smallest / len(pieces), top_value / len(pieces)))
        gain = gain * jnp.repeat(steps, shape[position] // parts).reshape([-1 if axis == position else 1 for axis in range(len(shape))])
    return gain


def scatter_about(rng, extent, width, most, cuts=(), kind=jnp.bfloat16):
    factor_of = shard_levels(rng, extent, cuts, -0.22, 0.18) if cuts else 1.0
    result = jax.random.normal(rng, extent, jnp.float32) * width * factor_of
    return jnp.minimum(jnp.maximum(result, -most), most).astype(kind)


def setup_inputs(seed: int = 0) -> dict:
    key_of = jax.random.split(jax.random.key(seed), 3)
    start_vectors = scatter_about(key_of[0], (M, NZ, NY, NX), 1.0, 6.0, ((2, 8), (3, 2)), jnp.float32)
    potential = draw_potential(jax.random.fold_in(key_of[2], 71), 0)
    return {"start_vectors": start_vectors, "potential": potential}


diag_shift = 3.0
kinetic_half = 0.5
contour_centre = -1.0
contour_radius = 2.0

def contour(index):
    angle = math.pi * (jnp.asarray(index).astype(jnp.float32) + 0.5) / POINTS
    shift_real = contour_centre + contour_radius * jnp.cos(angle)
    shift_imag = contour_radius * jnp.sin(angle)
    weight_real = contour_radius / POINTS * jnp.cos(angle)
    weight_imag = contour_radius / POINTS * jnp.sin(angle)
    return (shift_real, shift_imag, weight_real, weight_imag)

def apply_hamiltonian(field, potential):
    near = jnp.roll(field, 1, -2) + jnp.roll(field, -1, -2)
    near = near + jnp.roll(field, 1, -1) + jnp.roll(field, -1, -1)
    zeros = jnp.zeros_like(field[..., :1, :, :])
    near = near + jnp.concatenate([zeros, field[..., :-1, :, :]], axis=-3) + jnp.concatenate([field[..., 1:, :, :], zeros], axis=-3)
    return (diag_shift + potential) * field - kinetic_half * near

def reference(start_vectors, potential):
    diagonal_term = diag_shift + potential

    def filter_one(vector):
        filtered = jnp.zeros_like(vector)
        for point in range(POINTS):
            shift_real, shift_imag, weight_real, weight_imag = contour(point)
            offset = shift_real - diagonal_term
            magnitude = offset * offset + shift_imag * shift_imag
            inverse_real = offset / magnitude
            inverse_imag = -shift_imag / magnitude
            real_part = jnp.zeros_like(vector)
            imag_part = jnp.zeros_like(vector)
            for iteration in range(ITERS):
                image_real = apply_hamiltonian(real_part, potential)
                image_imag = apply_hamiltonian(imag_part, potential)
                resid_real = vector - (shift_real * real_part - shift_imag * imag_part - image_real)
                resid_imag = -(shift_real * imag_part + shift_imag * real_part - image_imag)
                real_part, imag_part = (real_part + (inverse_real * resid_real - inverse_imag * resid_imag), imag_part + (inverse_real * resid_imag + inverse_imag * resid_real))
            filtered = filtered + (weight_real * real_part - weight_imag * imag_part)
        return filtered
    filtered = lax.map(filter_one, start_vectors)
    image = lax.map(lambda vector: apply_hamiltonian(vector, potential), filtered)
    flat = filtered.reshape(M, -1)
    image_flat = image.reshape(M, -1)
    cells = float(NX * NY * NZ)
    gram = jnp.dot(flat.astype(jnp.float32), flat.T.astype(jnp.float32), precision=lax.Precision.HIGHEST, preferred_element_type=jnp.float32) / cells
    image_gram = jnp.dot(flat.astype(jnp.float32), image_flat.T.astype(jnp.float32), precision=lax.Precision.HIGHEST, preferred_element_type=jnp.float32) / cells
    lower = jnp.linalg.cholesky(gram)
    identity = jnp.eye(M, dtype=jnp.float32)
    inverse = lax.linalg.triangular_solve(lower, identity, left_side=True, lower=True)
    basis = jnp.dot(inverse.astype(jnp.float32), flat.astype(jnp.float32), precision=lax.Precision.HIGHEST, preferred_element_type=jnp.float32)
    projected = jnp.dot(jnp.dot(inverse.astype(jnp.float32), image_gram.astype(jnp.float32), precision=lax.Precision.HIGHEST, preferred_element_type=jnp.float32).astype(jnp.float32), inverse.T.astype(jnp.float32), precision=lax.Precision.HIGHEST, preferred_element_type=jnp.float32)
    return (basis.reshape(filtered.shape), projected)
```

```python
import functools
import math

import jax
import jax.numpy as jnp
from jax import lax
from jax.experimental import pallas as pl
from jax.experimental.pallas import tpu as pltpu
from jax.sharding import PartitionSpec as P

POINTS = 4
ITERS = 3

diag_shift = 3.0
kinetic_half = 0.5
contour_centre = -1.0
contour_radius = 2.0

LANES = 128
SUB = 8
REACH = ITERS
GROUP = 16


def contour(index):
    angle = math.pi * (index + 0.5) / POINTS
    return (
        contour_centre + contour_radius * math.cos(angle),
        contour_radius * math.sin(angle),
        contour_radius / POINTS * math.cos(angle),
        contour_radius / POINTS * math.sin(angle),
    )


def coefficients(pot, index):
    shift_real, shift_imag, weight_real, weight_imag = contour(index)
    offset = shift_real - (diag_shift + pot)
    scale = 1.0 / (offset * offset + shift_imag * shift_imag)
    real = offset * scale
    imag = -shift_imag * scale
    return (
        kinetic_half * real,
        kinetic_half * imag,
        weight_real * real - weight_imag * imag,
        weight_real * imag + weight_imag * real,
    )


def lane_ids(shape=(SUB, LANES)):
    return lax.broadcasted_iota(jnp.int32, shape, len(shape) - 1)


def sub_ids():
    return lax.broadcasted_iota(jnp.int32, (SUB, LANES), 0)


def near_sums(above, here, below):
    out = []
    for z, value in enumerate(here):
        near = above[z] + below[z]
        near = near + (pltpu.roll(value, 1, 1) + pltpu.roll(value, LANES - 1, 1))
        if z > 0:
            near = near + here[z - 1]
        if z + 1 < len(here):
            near = near + here[z + 1]
        out.append(near)
    return out


def spread(ref, row):
    return ref[pl.ds(row, SUB, stride=0), :]


def strip_of(tile_at, nz):
    lane = lane_ids()
    col = lane % GROUP
    group = lane // GROUP
    low = (col >= REACH) & (col < 8)
    high = (col >= 8) & (col < 16 - REACH)
    out = jnp.zeros((SUB, LANES), jnp.float32)
    for z in range(nz):
        value = tile_at(z)
        first = pltpu.roll(value, (GROUP * z + REACH) % LANES, 1)
        last = pltpu.roll(value, (GROUP * z + 8 + 5) % LANES, 1)
        out = jnp.where(low & (group == z), first, out)
        out = jnp.where(high & (group == z), last, out)
    return out


def outer_lanes():
    col = lane_ids() % GROUP
    return (col < REACH) | (col >= GROUP - REACH)


def send_strip(strip):
    col = lane_ids() % GROUP
    return jnp.where(col < 8, pltpu.roll(strip, LANES - 10, 1), pltpu.roll(strip, 10, 1))


def pack_kernel(x_hbm, pot_ref, out_ref, buf, sem):
    cp = lax.axis_index("cp")
    rows = x_hbm.shape[1]
    nz = pot_ref.shape[0]
    vectors = x_hbm.shape[0] // nz
    copy = pltpu.make_async_copy(x_hbm.at[:, pl.ds(cp * (rows - SUB), SUB), :], buf, sem)
    copy.start()
    pot = pot_ref.reshape(nz * rows, LANES)
    for k in range(REACH):
        row = k + cp * (rows - 1 - 2 * k)
        out_ref[REACH * nz + k] = pot[pl.ds(row, nz, stride=rows), :]
    copy.wait()
    flat = buf.reshape(vectors * nz * SUB, LANES)
    for k in range(REACH):
        row = k + cp * (SUB - 1 - 2 * k)
        for z in range(nz):
            out_ref[k * nz + z] = flat[pl.ds(z * SUB + row, vectors, stride=nz * SUB), :]


def interior_kernel(
    x_hbm, pot_ref, part_ref, edge_ref, strip_ref, pot_strip_ref, xs, tab, ub, vb, sem
):
    cp = lax.axis_index("cp")
    rows = x_hbm.shape[1]
    nz = pot_ref.shape[0]
    vectors = x_hbm.shape[0] // nz
    height = xs.shape[1]
    local = rows // 2 + REACH
    copy = pltpu.make_async_copy(
        x_hbm.at[:, pl.ds(cp * (rows - height), height), :], xs, sem
    )
    copy.start()
    pot = pot_ref.reshape(nz * rows, LANES)
    table = tab.reshape(POINTS * 4 * local * nz, LANES)

    def fill(r, carry):
        tile = pot[pl.ds(r + cp * (rows - 1 - 2 * r), nz, stride=rows), :]
        for j in range(POINTS):
            for q, value in enumerate(coefficients(tile, j)):
                tab[(j * 4 + q) * local + r] = value
        return carry

    lax.fori_loop(0, local, fill, 0)
    copy.wait()
    flat = xs.reshape(vectors * nz * height, LANES)

    def x_at(r, z):
        return flat[pl.ds(z * height + (r + cp * (height - 1 - 2 * r)), vectors, stride=nz * height), :]

    def strips(r, carry):
        strip_ref[r] = strip_of(lambda z: x_at(r, z), nz)
        row = r + cp * (rows - 1 - 2 * r)
        pot_strip_ref[r] = strip_of(lambda z: spread(pot, z * rows + row), nz)
        return carry

    lax.fori_loop(0, local, strips, 0)

    def clear(r, carry):
        for z in range(nz):
            part_ref[r, z] = jnp.zeros((SUB, LANES), jnp.float32)
        return carry

    lax.fori_loop(0, part_ref.shape[0], clear, 0)

    def point(j, carry):
        def coef(q, r, z):
            return spread(table, ((j * 4 + q) * local + r) * nz + z)

        def first(r, inner):
            for z in range(nz):
                x = x_at(r, z)
                ub[0, r, z] = coef(0, r, z) * x
                ub[1, r, z] = coef(1, r, z) * x
            return inner

        lax.fori_loop(0, local, first, 0)

        def rows_of(ref, q, r):
            return [ref[q, r, z] for z in range(nz)]

        def second(r, inner):
            near = [
                near_sums(rows_of(ub, q, r - 1), rows_of(ub, q, r), rows_of(ub, q, r + 1))
                for q in range(2)
            ]
            for z in range(nz):
                rest = x_at(r, z) - near[0][z]
                real, imag = coef(0, r, z), coef(1, r, z)
                vb[0, r, z] = real * rest + imag * near[1][z]
                vb[1, r, z] = imag * rest - real * near[1][z]
            return inner

        lax.fori_loop(1, local - 1, second, 0)
        for r in range(1, REACH):
            for q in range(2):
                for z in range(nz):
                    edge_ref[j, q, r - 1, z] = vb[q, r, z]

        def third(r, inner):
            near = [
                near_sums(rows_of(vb, q, r - 1), rows_of(vb, q, r), rows_of(vb, q, r + 1))
                for q in range(2)
            ]
            for z in range(nz):
                add = coef(2, r, z) * (x_at(r, z) - near[0][z]) + coef(3, r, z) * near[1][z]
                part_ref[r - 2, z] = part_ref[r - 2, z] + add
            return inner

        lax.fori_loop(2, local - 2, third, 0)
        return carry

    lax.fori_loop(0, POINTS, point, 0)


def strip_kernel(recv_ref, strip_ref, pot_strip_ref, all_ref, pot_ref, send_ref, tmp):
    nz = recv_ref.shape[0] // REACH - 1
    local = strip_ref.shape[0]
    total = local + REACH
    sub = sub_ids()
    flat = recv_ref.reshape(recv_ref.shape[0] * SUB, LANES)
    pots = [jnp.zeros((SUB, LANES), jnp.float32) for _ in range(pot_ref.shape[0])]
    for ri in range(total):
        if ri < REACH:
            k = REACH - 1 - ri
            strip = strip_of(lambda z: recv_ref[k * nz + z], nz)
            pot = strip_of(lambda z: spread(flat, (REACH * nz + k) * SUB + z), nz)
        else:
            strip = strip_ref[ri - REACH]
            pot = pot_strip_ref[ri - REACH]
        all_ref[ri] = strip
        send_ref[ri] = send_strip(strip)
        pots[ri // SUB] = jnp.where(sub == ri % SUB, pot, pots[ri // SUB])
    for t, value in enumerate(pots):
        pot_ref[t] = value
        send_ref[total + t] = send_strip(value)


def border_kernel(own_ref, recv_ref, edge_ref, out_ref, tab, ub, vb):
    nz = own_ref.shape[0] // REACH - 1
    span = REACH + 2
    table = tab.reshape(4 * (span + 1) * nz, LANES)

    def x_at(r, z):
        return own_ref[r * nz + z] if r >= 0 else recv_ref[(-1 - r) * nz + z]

    for j in range(POINTS):
        for r in range(-REACH, 2):
            tile = own_ref[REACH * nz + r] if r >= 0 else recv_ref[REACH * nz - 1 - r]
            for q, value in enumerate(coefficients(tile, j)):
                tab[q * (span + 1) + r + REACH] = value

        def coef(q, r, z):
            return spread(table, (q * (span + 1) + r + REACH) * nz + z)

        for r in range(-REACH, 2):
            for z in range(nz):
                x = x_at(r, z)
                ub[0, r + REACH, z] = coef(0, r, z) * x
                ub[1, r + REACH, z] = coef(1, r, z) * x

        def rows_of(ref, q, r):
            return [ref[q, r + REACH, z] for z in range(nz)]

        for r in range(1 - REACH, 1):
            near = [
                near_sums(rows_of(ub, q, r - 1), rows_of(ub, q, r), rows_of(ub, q, r + 1))
                for q in range(2)
            ]
            for z in range(nz):
                rest = x_at(r, z) - near[0][z]
                real, imag = coef(0, r, z), coef(1, r, z)
                vb[0, r + REACH, z] = real * rest + imag * near[1][z]
                vb[1, r + REACH, z] = imag * rest - real * near[1][z]

        def later(q, r):
            if r >= 1:
                return [edge_ref[j, q, r - 1, z] for z in range(nz)]
            return rows_of(vb, q, r)

        for r in range(-1, 2):
            near = [near_sums(later(q, r - 1), later(q, r), later(q, r + 1)) for q in range(2)]
            for z in range(nz):
                add = coef(2, r, z) * (x_at(r, z) - near[0][z]) + coef(3, r, z) * near[1][z]
                if j == 0:
                    out_ref[r + 1, z] = add
                else:
                    out_ref[r + 1, z] = out_ref[r + 1, z] + add


def close_kernel(
    all_ref, pot_strip_ref, recv_ref, border_ref, part_ref, pot_ref,
    own_ref, packet_ref, tab, xb, ub, vb, fb, pb, sb,
):
    cp = lax.axis_index("cp")
    nz, rows, _ = pot_ref.shape
    half = rows // 2
    total = all_ref.shape[0]
    tiles = pot_strip_ref.shape[0]
    outer = outer_lanes()
    lane = lane_ids()
    pot = pot_ref.reshape(nz * rows, LANES)

    for ri in range(total):
        xb[ri] = jnp.where(outer, recv_ref[ri], all_ref[ri])
    for t in range(tiles):
        value = jnp.where(outer, recv_ref[total + t], pot_strip_ref[t])
        for j in range(POINTS):
            for q, item in enumerate(coefficients(value, j)):
                tab[(j * 4 + q) * tiles + t] = item
    table = tab.reshape(POINTS * 4 * tiles * SUB, LANES)

    def strip_near(ref, q, ri):
        value = ref[q, ri]
        near = ref[q, ri - 1] + ref[q, ri + 1]
        near = near + (pltpu.roll(value, 1, 1) + pltpu.roll(value, LANES - 1, 1))
        below = jnp.where(lane >= GROUP, pltpu.roll(value, GROUP, 1), 0.0)
        above = jnp.where(lane < (nz - 1) * GROUP, pltpu.roll(value, LANES - GROUP, 1), 0.0)
        return near + (below + above)

    def coef(j, q, ri):
        return spread(table, (j * 4 + q) * tiles * SUB + ri)

    for ri in range(2, total - 2):
        fb[ri] = jnp.zeros((SUB, LANES), jnp.float32)

    def point(j, carry):
        for ri in range(total):
            ub[0, ri] = coef(j, 0, ri) * xb[ri]
            ub[1, ri] = coef(j, 1, ri) * xb[ri]
        for ri in range(1, total - 1):
            near = [strip_near(ub, q, ri) for q in range(2)]
            rest = xb[ri] - near[0]
            real, imag = coef(j, 0, ri), coef(j, 1, ri)
            vb[0, ri] = real * rest + imag * near[1]
            vb[1, ri] = imag * rest - real * near[1]
        for ri in range(2, total - 2):
            near = [strip_near(vb, q, ri) for q in range(2)]
            fb[ri] = fb[ri] + (coef(j, 2, ri) * (xb[ri] - near[0]) + coef(j, 3, ri) * near[1])
        return carry

    lax.fori_loop(0, POINTS, point, 0)

    low = lane < REACH
    high = lane >= LANES - REACH

    def patch(r, value_at):
        strip = fb[r + REACH]
        for z in range(nz):
            right = pltpu.roll(strip, (LANES - GROUP * z - 13) % LANES, 1)
            left = pltpu.roll(strip, (2 * LANES - 1 - GROUP * z - 2) % LANES, 1)
            value = jnp.where(high, right, jnp.where(low, left, value_at(z)))
            pb[r + 1, z] = value
            sb[r + 1, z] = pltpu.roll(jnp.where(lane == LANES - 1, left, value), 1, 1) + pltpu.roll(
                jnp.where(lane == 0, right, value), LANES - 1, 1
            )

    for r in range(-1, 2):
        patch(r, lambda z: border_ref[r + 1, z])

    def patches(r, carry):
        patch(r, lambda z: part_ref[r - 2, z])
        return carry

    lax.fori_loop(2, half + 1, patches, 0)

    count = SUB // 2 + 1

    def sums(r, carry):
        grams, images = list(carry[0]), list(carry[1])
        row = r + cp * (rows - 1 - 2 * r)
        here = [pb[r + 1, z] for z in range(nz)]
        for z in range(nz):
            near = (pb[r, z] + pb[r + 2, z]) + sb[r + 1, z]
            if z > 0:
                near = near + here[z - 1]
            if z + 1 < nz:
                near = near + here[z + 1]
            value = here[z]
            image = (diag_shift + spread(pot, z * rows + row)) * value - kinetic_half * near
            own_ref[r + cp * (half - 1 - 2 * r), z] = value
            for s in range(count):
                other = value if s == 0 else pltpu.roll(value, SUB - s, 0)
                grams[s] = grams[s] + other * value
                images[s] = images[s] + other * image
        return tuple(grams), tuple(images)

    zero = tuple(jnp.zeros((SUB, LANES), jnp.float32) for _ in range(count))
    grams, images = lax.fori_loop(0, half, sums, (zero, zero))
    tile = jnp.zeros((SUB, LANES), jnp.float32)
    for s in range(count):
        tile = jnp.where(lane == s, jnp.sum(grams[s], axis=1, keepdims=True), tile)
        tile = jnp.where(lane == SUB + s, jnp.sum(images[s], axis=1, keepdims=True), tile)
    spun = pltpu.roll(tile, 0, 1, stride=GROUP, stride_axis=0)
    line = jnp.sum(spun, axis=0, keepdims=True)
    packet_ref[...] = jnp.broadcast_to(line[None], packet_ref.shape)


def finish_kernel(
    packet_ref, own_hbm, other_hbm, basis_ref, projected_ref, buf, splat, sems, *, cells
):
    cp = lax.axis_index("cp")
    half = own_hbm.shape[0]
    nz = own_hbm.shape[1]
    vectors = own_hbm.shape[2]
    copies = [
        pltpu.make_async_copy(own_hbm, buf.at[pl.ds(cp * half, half)], sems.at[0]),
        pltpu.make_async_copy(other_hbm, buf.at[pl.ds((1 - cp) * half, half)], sems.at[1]),
    ]
    for copy in copies:
        copy.start()
    lane = lane_ids()
    sub = sub_ids()
    line = jnp.sum(packet_ref[...], axis=0) / cells
    tile = jnp.where(lane // GROUP == sub, jnp.broadcast_to(line, (SUB, LANES)), 0.0)
    for shift in (4 * GROUP, 2 * GROUP, GROUP):
        tile = tile + pltpu.roll(tile, shift, 1)
    for s in range(SUB // 2 + 1, SUB):
        moved = pltpu.roll(pltpu.roll(tile, SUB - s, 0), 2 * s - SUB, 1)
        tile = jnp.where((lane == s) | (lane == SUB + s), moved, tile)

    def square(value):
        value = jnp.where(lane < SUB, value, 0.0)
        value = value + pltpu.roll(value, LANES - SUB, 1)
        return jnp.where(lane < SUB, pltpu.roll(value, 0, 1, stride=1, stride_axis=0), 0.0)

    gram = square(tile)
    image = square(pltpu.roll(tile, LANES - SUB, 1))
    work = gram + jnp.where(lane == sub + SUB, 1.0, 0.0) + pltpu.roll(image, 2 * SUB, 1)

    def column(value, k):
        return jnp.sum(jnp.where(lane == k, value, 0.0), axis=1, keepdims=True)

    root = jnp.zeros((SUB, 1), jnp.float32)
    ids = sub[:, :1]
    for k in range(SUB):
        pivot_row = work[k : k + 1, :]
        pivot = pivot_row[:, k : k + 1]
        root = jnp.where(ids == k, 1.0 / jnp.sqrt(pivot), root)
        factor = jnp.where(ids > k, column(work, k) / pivot, 0.0)
        work = work - factor * pivot_row
    work = work * root
    inverse = jnp.where(lane < SUB, pltpu.roll(work, LANES - SUB, 1), 0.0)
    mixed = jnp.where(lane < SUB, pltpu.roll(work, LANES - 2 * SUB, 1), 0.0)
    result = jnp.zeros((SUB, LANES), jnp.float32)
    for c in range(SUB):
        part = jnp.sum(mixed * inverse[c : c + 1, :], axis=1, keepdims=True)
        result = jnp.where(lane == c, part, result)
    projected_ref[...] = result[:, :SUB]
    for b in range(SUB):
        splat[b] = jnp.broadcast_to(column(inverse, b), (SUB, LANES))
    splats = splat.reshape(SUB * SUB, LANES)
    weights = [[spread(splats, b * SUB + a) for b in range(a + 1)] for a in range(vectors)]
    for copy in copies:
        copy.wait()
    flat = buf.reshape(2 * half * nz * vectors, LANES)

    def plane(z, carry):
        for block in range(2 * half // SUB):
            loads = [
                flat[pl.ds((block * SUB * nz + z) * vectors + b, SUB, stride=nz * vectors), :]
                for b in range(vectors)
            ]
            for a in range(vectors):
                value = weights[a][0] * loads[0]
                for b in range(1, a + 1):
                    value = value + weights[a][b] * loads[b]
                basis_ref[a, z, block * SUB : (block + 1) * SUB, :] = value
        return carry

    lax.fori_loop(0, nz, plane, 0)


def call(kernel, operands, outs, scratch, spaces, flops=0, **options):
    return pl.pallas_call(
        functools.partial(kernel, **options),
        out_shape=[jax.ShapeDtypeStruct(shape, jnp.float32) for shape in outs],
        in_specs=[pl.BlockSpec(memory_space=space) for space in spaces],
        out_specs=[pl.BlockSpec(memory_space=pltpu.VMEM) for _ in outs],
        scratch_shapes=scratch,
        cost_estimate=pl.CostEstimate(
            flops=flops,
            bytes_accessed=sum(value.size * 4 for value in operands)
            + sum(4 * math.prod(shape) for shape in outs),
            transcendentals=0,
        ),
    )(*operands)


def per_device(start_vectors, potential):
    vectors, nz, rows, columns = start_vectors.shape
    half = rows // 2
    local = half + REACH
    total = local + REACH
    height = -(-local // SUB) * SUB
    assert vectors == SUB and nz == SUB and columns == LANES
    assert lax.axis_size("cp") == 2 and rows % SUB == 0
    vmem, far = pltpu.VMEM, pl.ANY
    tile = (SUB, LANES)
    f32 = jnp.float32
    flat = start_vectors.reshape(vectors * nz, rows, columns)

    count = lax.axis_size("gy")
    swaps = []
    for g in range(count):
        swaps.append((2 * g, 2 * ((g - 1) % count) + 1))
        swaps.append((2 * g + 1, 2 * ((g + 1) % count)))
    (own_rows,) = call(
        pack_kernel, (flat, potential), [(REACH * (nz + 1),) + tile],
        [pltpu.VMEM((vectors * nz, SUB, LANES), f32), pltpu.SemaphoreType.DMA],
        (far, vmem),
    )
    far_rows = lax.ppermute(own_rows, ("gy", "cp"), swaps)
    part, edge, strip, pot_strip = call(
        interior_kernel, (flat, potential),
        [(local - 4, nz) + tile, (POINTS, 2, REACH - 1, nz) + tile, (local,) + tile, (local,) + tile],
        [
            pltpu.VMEM((vectors * nz, height, LANES), f32),
            pltpu.VMEM((POINTS * 4 * local,) + tile, f32),
            pltpu.VMEM((2, local, nz) + tile, f32),
            pltpu.VMEM((2, local, nz) + tile, f32),
            pltpu.SemaphoreType.DMA,
        ],
        (far, vmem), flops=10**8,
    )
    tiles = -(-total // SUB)
    strips, pot_strips, send = call(
        strip_kernel, (far_rows, strip, pot_strip),
        [(total,) + tile, (tiles,) + tile, (total + tiles,) + tile],
        [pltpu.VMEM(tile, f32)], (vmem,) * 3,
    )
    size = lax.axis_size("gx")
    ahead = [(i, (i + 1) % size) for i in range(size)]
    back = [(i, (i - 1) % size) for i in range(size)]
    recv = lax.ppermute(send, "gx", ahead)
    if size > 2:
        other = lax.ppermute(send, "gx", back)
        recv = jnp.where((jnp.arange(LANES) % GROUP) < GROUP // 2, recv, other)
    (border,) = call(
        border_kernel, (own_rows, far_rows, edge), [(REACH, nz) + tile],
        [
            pltpu.VMEM((4 * (REACH + 3),) + tile, f32),
            pltpu.VMEM((2, REACH + 3, nz) + tile, f32),
            pltpu.VMEM((2, REACH + 3, nz) + tile, f32),
        ],
        (vmem,) * 3, flops=3 * 10**7,
    )
    axes = ("gx", "gy", "cp")
    devices = math.prod(lax.axis_size(axis) for axis in axes)
    own, packet = call(
        close_kernel, (strips, pot_strips, recv, border, part, potential),
        [(half, nz) + tile, (devices, 1, LANES)],
        [
            pltpu.VMEM((POINTS * 4 * tiles,) + tile, f32),
            pltpu.VMEM((total,) + tile, f32),
            pltpu.VMEM((2, total) + tile, f32),
            pltpu.VMEM((2, total) + tile, f32),
            pltpu.VMEM((total,) + tile, f32),
            pltpu.VMEM((half + 2, nz) + tile, f32),
            pltpu.VMEM((half + 2, nz) + tile, f32),
        ],
        (vmem,) * 6, flops=10**7,
    )
    other = lax.ppermute(own, "cp", [(0, 1), (1, 0)])
    packets = lax.all_to_all(packet, axes, 0, 0, tiled=True)
    cells = float(nz * rows * columns * lax.axis_size("gx") * lax.axis_size("gy"))
    basis, projected = call(
        finish_kernel, (packets, own, other),
        [(vectors, nz, rows, columns), (vectors, vectors)],
        [
            pltpu.VMEM((rows, nz) + tile, f32),
            pltpu.VMEM((SUB,) + tile, f32),
            pltpu.SemaphoreType.DMA((2,)),
        ],
        (vmem, far, far), cells=cells,
    )
    return (basis, projected)


def solution(mesh):
    in_specs = (P(None, None, "gy", "gx"), P(None, "gy", "gx"))
    out_specs = (P(None, None, "gy", "gx"), P())
    return jax.shard_map(
        per_device, mesh=mesh, in_specs=in_specs, out_specs=out_specs, check_vma=False
    )
```

```python
import functools
import math

import jax
import jax.numpy as jnp
from jax import lax
from jax.experimental import pallas as pl
from jax.experimental.pallas import tpu as pltpu
from jax.sharding import PartitionSpec as P

POINTS = 4
ITERS = 3

diag_shift = 3.0
kinetic_half = 0.5
contour_centre = -1.0
contour_radius = 2.0

LANES = 128
SUB = 8
REACH = ITERS
GROUP = 16
GRANT = 16 * 2**20
TABLES = 12
EDGE = 2


def contour(index):
    angle = math.pi * (index + 0.5) / POINTS
    return (
        contour_centre + contour_radius * math.cos(angle),
        contour_radius * math.sin(angle),
        contour_radius / POINTS * math.cos(angle),
        contour_radius / POINTS * math.sin(angle),
    )


def coefficients(pot, index):
    shift_real, shift_imag, weight_real, weight_imag = contour(index)
    offset = shift_real - (diag_shift + pot)
    scale = 1.0 / (offset * offset + shift_imag * shift_imag)
    real = offset * scale
    imag = -shift_imag * scale
    return (
        kinetic_half * real,
        kinetic_half * imag,
        weight_real * real - weight_imag * imag,
        weight_real * imag + weight_imag * real,
    )


def lane_ids():
    return lax.broadcasted_iota(jnp.int32, (SUB, LANES), 1)


def sub_ids():
    return lax.broadcasted_iota(jnp.int32, (SUB, LANES), 0)


def turn(value, shift):
    return pltpu.roll(value, shift % LANES, 1)


def spread(ref, row):
    return ref[pl.ds(row, SUB, stride=0), :]


def all_sublanes(value):
    for shift in (4, 2, 1):
        value = value + pltpu.roll(value, shift, 0)
    return value


def column_ids():
    return lane_ids() & (GROUP - 1)


def settle(packed):
    col = column_ids()
    low = (col >= REACH) & (col < 8)
    high = (col >= 8) & (col < GROUP - REACH)
    return jnp.where(low, packed, jnp.where(high, turn(packed, 10), 0.0))


def strip_of(tiles):
    lane = lane_ids()
    packed = jnp.zeros((SUB, LANES), jnp.float32)
    for z, value in enumerate(tiles):
        inside = ((lane + 2 - GROUP * z) & (LANES - 1)) < 10
        packed = jnp.where(inside, turn(value, GROUP * z + REACH), packed)
    return settle(packed)


def strip_of_layers(tile):
    moved = pltpu.roll(tile, REACH, 1, stride=GROUP, stride_axis=0)
    inside = ((lane_ids() + 2 - GROUP * sub_ids()) & (LANES - 1)) < 10
    return settle(all_sublanes(jnp.where(inside, moved, 0.0)))


def outer_lanes():
    col = column_ids()
    return (col < REACH) | (col >= GROUP - REACH)


def send_strip(strip):
    return jnp.where(column_ids() < 8, turn(strip, -10), turn(strip, 10))


def copy_rows(x_hbm, window, sems, height, cp):
    rows = x_hbm.shape[2]
    return [
        pltpu.make_async_copy(
            x_hbm.at[v, :, pl.ds(cp * (rows - height), height), :], window.at[:, v], sems.at[v]
        )
        for v in range(x_hbm.shape[0])
    ]


def pack_kernel(x_hbm, pot_hbm, out_ref, window, pot_buf, sems):
    cp = lax.axis_index("cp")
    vectors, nz, rows, _ = x_hbm.shape
    offset = cp * (rows - SUB)
    copies = copy_rows(x_hbm, window, sems, SUB, cp)
    copies.append(
        pltpu.make_async_copy(pot_hbm.at[:, pl.ds(offset, SUB), :], pot_buf, sems.at[vectors])
    )
    for copy in copies:
        copy.start()
    for copy in copies:
        copy.wait()
    flat = window.reshape(nz * vectors * SUB, LANES)
    pot = pot_buf.reshape(nz * SUB, LANES)
    for k in range(REACH):
        row = k + cp * (SUB - 1 - 2 * k)
        for z in range(nz):
            out_ref[k * nz + z] = flat[pl.ds(z * vectors * SUB + row, vectors, stride=SUB), :]
        out_ref[REACH * nz + k] = pot[pl.ds(row, nz, stride=SUB), :]


def add(total, value):
    return value if total is None else total + value


def fill_tables(tab, tile, slot):
    total = None
    sides = (tile, turn(tile, 1), turn(tile, -1))
    for j in range(POINTS):
        for d, side in enumerate(sides):
            values = coefficients(side, j)
            for q, value in enumerate(values):
                tab[slot(j * TABLES + 4 * d + q)] = value
            if d == 0:
                total = add(total, values[2])
    tab[slot(POINTS * TABLES)] = total


def first_step(coef, x, ub, r, nz):
    for z in range(nz):
        for j in range(POINTS):
            for q in range(2):
                ub[j, q, r, z] = coef(j, q, z) * x[z]


def cross(rows, z):
    above, here, below = rows
    near = above[z] + below[z]
    if z > 0:
        near = near + here[z - 1]
    if z + 1 < len(here):
        near = near + here[z + 1]
    return near


def second_step(coef, x, left, right, rows_of, store, nz):
    for j in range(POINTS):
        rows = [rows_of(j, q) for q in range(2)]
        for z in range(nz):
            near = [
                cross(rows[q], z)
                + (coef(j, 4 + q, z) * left[z] + coef(j, 8 + q, z) * right[z])
                for q in range(2)
            ]
            rest = x[z] - near[0]
            real, imag = coef(j, 0, z), coef(j, 1, z)
            store(j, 0, z, real * rest + imag * near[1])
            store(j, 1, z, imag * rest - real * near[1])


def third_step(coef, x, rows_of, nz):
    straight, ahead, back = [None] * nz, [None] * nz, [None] * nz
    for j in range(POINTS):
        rows = [rows_of(j, q) for q in range(2)]
        for z in range(nz):
            real, imag = rows[0][1][z], rows[1][1][z]
            straight[z] = add(
                straight[z],
                coef(j, 3, z) * cross(rows[1], z) - coef(j, 2, z) * cross(rows[0], z),
            )
            ahead[z] = add(ahead[z], coef(j, 11, z) * imag - coef(j, 10, z) * real)
            back[z] = add(back[z], coef(j, 7, z) * imag - coef(j, 6, z) * real)
    return [
        (coef(POINTS, 0, z) * x[z] + straight[z]) + (turn(ahead[z], 1) + turn(back[z], -1))
        for z in range(nz)
    ]


def interior_kernel(
    x_ref, pot_ref, part_ref, edge_ref, strip_ref, pot_strip_ref, window, xs, tab, ub, vb, sems
):
    cp = lax.axis_index("cp")
    vectors, nz, rows, _ = x_ref.shape
    height = window.shape[2]
    local = rows // 2 + REACH
    span = xs.shape[1]
    copies = copy_rows(x_ref, window, sems, height, cp)
    for copy in copies:
        copy.start()
    pot = pot_ref.reshape(nz * rows, LANES)
    table = tab.reshape((POINTS * TABLES + 1) * span * nz, LANES)
    for copy in copies:
        copy.wait()
    flat = window.reshape(nz * vectors * height, LANES)

    def coefs(r):
        def coef(j, q, z):
            return spread(table, ((j * TABLES + q) * span + r) * nz + z)

        return coef

    for r in range(local):
        tile = pot[pl.ds(r + cp * (rows - 1 - 2 * r), nz, stride=rows), :]
        fill_tables(tab, tile, lambda index: index * span + r)
        pot_strip_ref[r] = strip_of_layers(tile)
        tiles = []
        for z in range(nz):
            start = z * vectors * height + r + cp * (height - 1 - 2 * r)
            value = flat[pl.ds(start, vectors, stride=height), :]
            xs[0, r, z] = value
            xs[1, r, z] = turn(value, 1)
            xs[2, r, z] = turn(value, -1)
            tiles.append(value)
        strip_ref[r] = strip_of(tiles)

    def x_at(r, d=0):
        return [xs[d, r, z] for z in range(nz)]

    def around(ref, r):
        return lambda j, q: [[ref[j, q, r + d, z] for z in range(nz)] for d in (-1, 0, 1)]

    for r in range(local):
        first_step(coefs(r), x_at(r), ub, r, nz)

    def second(r, carry):
        def store(j, q, z, value):
            vb[j, q, r, z] = value

        second_step(coefs(r), x_at(r), x_at(r, 1), x_at(r, 2), around(ub, r), store, nz)
        return carry

    lax.fori_loop(1, local - 1, second, 0)
    for j in range(POINTS):
        for q in range(2):
            for r in range(1, REACH):
                for z in range(nz):
                    edge_ref[j, q, r - 1, z] = vb[j, q, r, z]

    def third(r, carry):
        for z, value in enumerate(third_step(coefs(r), x_at(r), around(vb, r), nz)):
            part_ref[r - 2, z] = value
        return carry

    lax.fori_loop(2, local - 2, third, 0)


def strip_kernel(recv_ref, strip_ref, pot_strip_ref, all_ref, pot_ref, send_ref):
    nz = recv_ref.shape[0] // REACH - 1
    local = strip_ref.shape[0]
    total = local + REACH
    pairs = total // 2
    sub = sub_ids()
    outer = outer_lanes()
    pots = [jnp.zeros((SUB, LANES), jnp.float32) for _ in range(pot_ref.shape[0])]
    sends = []
    for ri in range(total):
        if ri < REACH:
            k = REACH - 1 - ri
            strip = strip_of([recv_ref[k * nz + z] for z in range(nz)])
            pot = strip_of_layers(recv_ref[REACH * nz + k])
        else:
            strip = strip_ref[ri - REACH]
            pot = pot_strip_ref[ri - REACH]
        all_ref[ri] = strip
        sends.append(send_strip(strip))
        pots[ri // SUB] = jnp.where(sub == ri % SUB, pot, pots[ri // SUB])
    for ri in range(pairs):
        send_ref[ri] = jnp.where(outer, sends[ri], turn(sends[ri + pairs], 8))
    for t, value in enumerate(pots):
        pot_ref[t] = value
        send_ref[pairs + t] = send_strip(value)


def gram_sums(other_of, value, image, grams, images):
    for s in range(len(grams)):
        other = other_of if s == 0 else pltpu.roll(other_of, SUB - s, 0)
        grams[s] = add(grams[s], other * value)
        images[s] = add(images[s], other * image)


def border_kernel(
    own_ref, recv_ref, edge_ref, part_ref, pot_ref, out_ref, sums_ref, tab, xs, ub, vb
):
    cp = lax.axis_index("cp")
    nz, rows, _ = pot_ref.shape
    half = rows // 2
    span = REACH + 2
    table = tab.reshape((POINTS * TABLES + 1) * span * nz, LANES)

    def coefs(r):
        def coef(j, q, z):
            return spread(table, ((j * TABLES + q) * span + r + REACH) * nz + z)

        return coef

    def x_at(r):
        return [own_ref[r * nz + z] if r >= 0 else recv_ref[(-1 - r) * nz + z] for z in range(nz)]

    def around(ref, r):
        def one(j, q, row):
            if row >= 1 and ref is vb:
                return [edge_ref[j, q, row - 1, z] for z in range(nz)]
            return [ref[j, q, row + REACH, z] for z in range(nz)]

        return lambda j, q: [one(j, q, r + d) for d in (-1, 0, 1)]

    for r in range(-REACH, 2):
        tile = own_ref[REACH * nz + r] if r >= 0 else recv_ref[REACH * nz - 1 - r]
        fill_tables(tab, tile, lambda index: index * span + r + REACH)
    for r in range(-REACH, 2):
        first_step(coefs(r), x_at(r), ub, r + REACH, nz)
    for r in range(1 - REACH, 1):
        def store(j, q, z, value):
            vb[j, q, r + REACH, z] = value

        x = x_at(r)
        left = [turn(value, 1) for value in x]
        right = [turn(value, -1) for value in x]
        second_step(coefs(r), x, left, right, around(ub, r), store, nz)
    for r in range(-1, 2):
        for z, value in enumerate(third_step(coefs(r), x_at(r), around(vb, r), nz)):
            out_ref[r + 1, z] = value

    lane = lane_ids()
    kept = (lane >= EDGE) & (lane < LANES - EDGE)
    pot = pot_ref.reshape(nz * rows, LANES)
    count = SUB // 2 + 1
    grams, images = [None] * count, [None] * count

    def row_of(r):
        return [out_ref[r + 1, z] if r < 2 else part_ref[r - 2, z] for z in range(nz)]

    for r in range(half):
        row = r + cp * (rows - 1 - 2 * r)
        above, below = row_of(r - 1), row_of(r + 1)
        here = [jnp.where(kept, value, 0.0) for value in row_of(r)]
        for z in range(nz):
            value = here[z]
            near = cross((above, here, below), z) + (turn(value, 1) + turn(value, -1))
            image = (diag_shift + spread(pot, z * rows + row)) * value - kinetic_half * near
            gram_sums(value, value, image, grams, images)
    for s, value in enumerate(grams + images):
        sums_ref[s] = value


def close_kernel(
    all_ref, pot_strip_ref, recv_ref, border_ref, part_ref, sums_ref,
    own_ref, packet_ref, tab, xb, ub, vb, fb,
):
    cp = lax.axis_index("cp")
    nz, half = own_ref.shape[:2]
    total = all_ref.shape[0]
    pairs = total // 2
    tiles = pot_strip_ref.shape[0]
    lane = lane_ids()
    col = column_ids()
    outer = outer_lanes()
    lower = lane >= GROUP
    upper = lane < (nz - 1) * GROUP
    shifts = (0, 1, -1, GROUP, -GROUP)
    span = tiles * SUB

    for t in range(tiles):
        value = jnp.where(outer, recv_ref[pairs + t], pot_strip_ref[t])
        pot_strip = value
        tab[POINTS * 20 * tiles + t] = pot_strip
        for d, shift in enumerate(shifts):
            side = value if d == 0 else turn(value, shift)
            for j in range(POINTS):
                for q, item in enumerate(coefficients(side, j)):
                    tab[(j * 20 + d * 4 + q) * tiles + t] = item
    table = tab.reshape((POINTS * 20 + 1) * span, LANES)

    def coef(j, d, q, ri):
        return spread(table, (j * 20 + d * 4 + q) * span + ri)

    for ri in range(total):
        came = recv_ref[ri] if ri < pairs else turn(recv_ref[ri - pairs], -8)
        value = jnp.where(outer, came, all_ref[ri])
        xb[0, ri] = value
        if 1 <= ri < total - 1:
            xb[1, ri] = turn(value, 1)
            xb[2, ri] = turn(value, -1)
            xb[3, ri] = jnp.where(lower, turn(value, GROUP), 0.0)
            xb[4, ri] = jnp.where(upper, turn(value, -GROUP), 0.0)
        for j in range(POINTS):
            for q in range(2):
                ub[j, q, ri] = coef(j, 0, q, ri) * value

    for ri in range(1, total - 1):
        sides = [xb[d, ri] for d in range(5)]
        for j in range(POINTS):
            near = []
            for q in range(2):
                value = ub[j, q, ri - 1] + ub[j, q, ri + 1]
                for d in range(1, 5):
                    value = value + coef(j, d, q, ri) * sides[d]
                near.append(value)
            rest = sides[0] - near[0]
            real, imag = coef(j, 0, 0, ri), coef(j, 0, 1, ri)
            vb[j, 0, ri] = real * rest + imag * near[1]
            vb[j, 1, ri] = imag * rest - real * near[1]

    for ri in range(2, total - 2):
        parts = [None] * 5
        weight = None
        for j in range(POINTS):
            weight = add(weight, coef(j, 0, 2, ri))
            for d in range(5):
                if d == 0:
                    real, imag = [vb[j, q, ri - 1] + vb[j, q, ri + 1] for q in range(2)]
                else:
                    real, imag = vb[j, 0, ri], vb[j, 1, ri]
                parts[d] = add(parts[d], coef(j, d, 3, ri) * imag - coef(j, d, 2, ri) * real)
        value = weight * xb[0, ri] + parts[0]
        value = value + (turn(parts[1], -1) + turn(parts[2], 1))
        value = value + jnp.where(upper, turn(parts[3], -GROUP), 0.0)
        fb[ri] = value + jnp.where(lower, turn(parts[4], GROUP), 0.0)

    count = SUB // 2 + 1
    grams = [sums_ref[s] for s in range(count)]
    images = [sums_ref[count + s] for s in range(count)]
    whole = ((col >= REACH) & (col < REACH + EDGE)) | (
        (col >= GROUP - REACH - EDGE) & (col < GROUP - REACH)
    )
    edge = (lane < EDGE) | (lane >= LANES - EDGE)
    joined = (col >= GROUP - REACH) & (col < GROUP - REACH + EDGE)
    for r in range(half):
        ri = r + REACH
        value = fb[ri]
        left, right = turn(value, 1), turn(value, -1)
        near = (fb[ri - 1] + fb[ri + 1]) + (left + right)
        near = near + jnp.where(lower, turn(value, GROUP), 0.0)
        near = near + jnp.where(upper, turn(value, -GROUP), 0.0)
        pot = spread(table, POINTS * 20 * span + ri)
        image = (diag_shift + pot) * value - kinetic_half * near
        rest = jnp.where(
            col == REACH + EDGE, left, jnp.where(col == GROUP - REACH - EDGE - 1, right, 0.0)
        )
        image = jnp.where(whole, image, -kinetic_half * rest)
        gram_sums(value, jnp.where(whole, value, 0.0), image, grams, images)
        compact = jnp.where(joined, turn(value, 10), value)
        place = r + cp * (half - 1 - 2 * r)
        for z in range(nz):
            base = border_ref[r + 1, z] if r < 2 else part_ref[r - 2, z]
            moved = turn(compact, -EDGE - GROUP * z - (GROUP - REACH - EDGE))
            own_ref[z, place] = jnp.where(edge, moved, base)

    tile = jnp.zeros((SUB, LANES), jnp.float32)
    for s in range(count):
        tile = jnp.where(lane == s, jnp.sum(grams[s], axis=1, keepdims=True), tile)
        tile = jnp.where(lane == SUB + s, jnp.sum(images[s], axis=1, keepdims=True), tile)
    spun = pltpu.roll(tile, 0, 1, stride=GROUP, stride_axis=0)
    line = jnp.sum(spun, axis=0, keepdims=True)
    packet_ref[...] = jnp.broadcast_to(line[None], packet_ref.shape)


def factor_inverse(entry, size):
    work = [[entry(i, k) for k in range(i + 1)] for i in range(size)]
    root = []
    for k in range(size):
        root.append(lax.rsqrt(work[k][k]))
        for i in range(k + 1, size):
            work[i][k] = work[i][k] * root[k]
        for i in range(k + 1, size):
            for m in range(k + 1, i + 1):
                work[i][m] = work[i][m] - work[i][k] * work[m][k]
    inverse = [[None] * (i + 1) for i in range(size)]
    for i in range(size):
        inverse[i][i] = root[i]
        for k in range(i):
            total = None
            for m in range(k, i):
                total = add(total, work[i][m] * inverse[m][k])
            inverse[i][k] = -(total * root[i])
    return inverse


def finish_kernel(packet_ref, own_ref, other_ref, basis_hbm, projected_ref, buf, out, sems, *, cells):
    cp = lax.axis_index("cp")
    nz, half = own_ref.shape[:2]
    vectors = basis_hbm.shape[0]
    own_copy = pltpu.make_async_copy(own_ref, buf.at[:, pl.ds(cp * half, half)], sems.at[0])
    other_copy = pltpu.make_async_copy(
        other_ref, buf.at[:, pl.ds((1 - cp) * half, half)], sems.at[1]
    )
    own_copy.start()
    other_copy.start()
    lane = lane_ids()
    sub = sub_ids()
    line = packet_ref[0:SUB, :]
    for start in range(SUB, packet_ref.shape[0], SUB):
        line = line + packet_ref[start : start + SUB, :]
    line = all_sublanes(line) * (1.0 / cells)

    def entry(i, k):
        s = (i - k) % SUB
        at = GROUP * k + s if s <= SUB // 2 else GROUP * i + SUB - s
        return jnp.broadcast_to(line[:, at : at + 1], (SUB, LANES))

    inverse = factor_inverse(entry, vectors)
    own_copy.wait()
    other_copy.wait()
    flat = buf.reshape(nz * 2 * half * vectors, LANES)
    copies = []
    for z in range(nz):
        for block in range(2 * half // SUB):
            loads = [
                flat[pl.ds((z * 2 * half + block * SUB) * vectors + b, SUB, stride=vectors), :]
                for b in range(vectors)
            ]
            for a in range(vectors):
                value = None
                for b in range(a + 1):
                    value = add(value, inverse[a][b] * loads[b])
                out[a, z, block * SUB : (block + 1) * SUB, :] = value
        copies.append(pltpu.make_async_copy(out.at[:, z], basis_hbm.at[:, z], sems.at[2 + z]))
        copies[-1].start()

    tile = jnp.where((lane >> 4) == sub, line, 0.0)
    for shift in (4 * GROUP, 2 * GROUP, GROUP):
        tile = tile + turn(tile, shift)
    tile = turn(tile, -SUB)
    for s in range(SUB // 2 + 1, SUB):
        moved = turn(pltpu.roll(tile, SUB - s, 0), 2 * s - SUB)
        tile = jnp.where(lane == s, moved, tile)
    tile = jnp.where(lane < SUB, tile, 0.0)
    tile = tile + turn(tile, -SUB)
    image = jnp.where(lane < SUB, pltpu.roll(tile, 0, 1, stride=1, stride_axis=0), 0.0)
    whole = jnp.zeros((SUB, LANES), jnp.float32)
    mixed = None
    for b in range(vectors):
        column = jnp.zeros((SUB, LANES), jnp.float32)
        for a in range(b, vectors):
            column = jnp.where(sub == a, inverse[a][b], column)
        whole = jnp.where(lane == b, column, whole)
        mixed = add(mixed, column * image[b : b + 1, :])
    result = jnp.zeros((SUB, LANES), jnp.float32)
    for c in range(vectors):
        part = jnp.sum(mixed * whole[c : c + 1, :], axis=1, keepdims=True)
        result = jnp.where(lane == c, part, result)
    projected_ref[...] = result[:, :vectors]
    for copy in copies:
        copy.wait()


def call(kernel, operands, outs, scratch, spaces, flops=0, out_spaces=None, **options):
    return pl.pallas_call(
        functools.partial(kernel, **options),
        out_shape=[jax.ShapeDtypeStruct(shape, jnp.float32) for shape in outs],
        in_specs=[pl.BlockSpec(memory_space=space) for space in spaces],
        out_specs=[
            pl.BlockSpec(memory_space=space) for space in out_spaces or [pltpu.VMEM] * len(outs)
        ],
        scratch_shapes=scratch,
        compiler_params=pltpu.CompilerParams(vmem_limit_bytes=GRANT),
        cost_estimate=pl.CostEstimate(
            flops=flops,
            bytes_accessed=sum(value.size * 4 for value in operands)
            + sum(4 * math.prod(shape) for shape in outs),
            transcendentals=0,
        ),
    )(*operands)


def per_device(start_vectors, potential):
    vectors, nz, rows, columns = start_vectors.shape
    half = rows // 2
    local = half + REACH
    total = local + REACH
    height = -(-local // SUB) * SUB
    assert vectors == SUB and nz == SUB and columns == LANES
    assert lax.axis_size("cp") == 2 and rows % SUB == 0 and total % 2 == 0
    vmem, far, hbm = pltpu.VMEM, pl.ANY, pltpu.HBM
    tile = (SUB, LANES)

    def room(*shape):
        return pltpu.VMEM(shape + tile, jnp.float32)

    count = lax.axis_size("gy")
    swaps = []
    for g in range(count):
        swaps.append((2 * g, 2 * ((g - 1) % count) + 1))
        swaps.append((2 * g + 1, 2 * ((g + 1) % count)))
    (own_rows,) = call(
        pack_kernel, (start_vectors, potential), [(REACH * (nz + 1),) + tile],
        [room(nz, vectors), room(nz), pltpu.SemaphoreType.DMA((vectors + 1,))],
        (hbm, hbm),
    )
    far_rows = lax.ppermute(own_rows, ("gy", "cp"), swaps)
    tables = POINTS * TABLES + 1
    part, edge, strip, pot_strip = call(
        interior_kernel, (start_vectors, potential),
        [(local - 4, nz) + tile, (POINTS, 2, REACH - 1, nz) + tile, (local,) + tile, (local,) + tile],
        [
            pltpu.VMEM((nz, vectors, height, LANES), jnp.float32),
            room(3, local + 2, nz),
            room(tables * (local + 2)),
            room(POINTS, 2, local + 2, nz),
            room(POINTS, 2, local, nz),
            pltpu.SemaphoreType.DMA((vectors,)),
        ],
        (far, vmem), flops=10**8,
    )
    tiles = -(-total // SUB)
    strips, pot_strips, send = call(
        strip_kernel, (far_rows, strip, pot_strip),
        [(total,) + tile, (tiles,) + tile, (total // 2 + tiles,) + tile],
        [], (vmem,) * 3,
    )
    size = lax.axis_size("gx")
    ahead = [(i, (i + 1) % size) for i in range(size)]
    back = [(i, (i - 1) % size) for i in range(size)]
    recv = lax.ppermute(send, "gx", ahead)
    if size > 2:
        other = lax.ppermute(send, "gx", back)
        recv = jnp.where((jnp.arange(LANES) % 8) < 4, recv, other)
    sums = 2 * (SUB // 2 + 1)
    border, partial = call(
        border_kernel, (own_rows, far_rows, edge, part, potential),
        [(REACH, nz) + tile, (sums,) + tile],
        [
            room(tables * (REACH + 2)),
            room(1),
            room(POINTS, 2, REACH + 2, nz),
            room(POINTS, 2, REACH + 2, nz),
        ],
        (vmem,) * 5, flops=3 * 10**7,
    )
    axes = ("gx", "gy", "cp")
    devices = math.prod(lax.axis_size(axis) for axis in axes)
    own, packet = call(
        close_kernel, (strips, pot_strips, recv, border, part, partial),
        [(nz, half) + tile, (devices, 1, LANES)],
        [
            room((POINTS * 20 + 1) * tiles),
            room(5, total),
            room(POINTS, 2, total),
            room(POINTS, 2, total),
            room(total),
        ],
        (vmem,) * 6, flops=10**7,
    )
    other = lax.ppermute(own, "cp", [(0, 1), (1, 0)])
    packets = lax.all_to_all(packet, axes, 0, 0, tiled=True).reshape(devices, LANES)
    cells = float(nz * rows * columns * lax.axis_size("gx") * lax.axis_size("gy"))
    basis, projected = call(
        finish_kernel, (packets, own, other),
        [(vectors, nz, rows, columns), (vectors, vectors)],
        [
            room(nz, rows),
            pltpu.VMEM((vectors, nz, rows, columns), jnp.float32),
            pltpu.SemaphoreType.DMA((2 + nz,)),
        ],
        (vmem, vmem, vmem), out_spaces=(hbm, vmem), cells=cells,
    )
    return (basis, projected)


def solution(mesh):
    in_specs = (P(None, None, "gy", "gx"), P(None, "gy", "gx"))
    out_specs = (P(None, None, "gy", "gx"), P())
    return jax.shard_map(
        per_device, mesh=mesh, in_specs=in_specs, out_specs=out_specs, check_vma=False
    )
```

```python
import functools
import math

import jax
import jax.numpy as jnp
from jax import lax
from jax.experimental import pallas as pl
from jax.experimental.pallas import tpu as pltpu
from jax.sharding import PartitionSpec as P

POINTS = 4
ITERS = 3

diag_shift = 3.0
kinetic_half = 0.5
contour_centre = -1.0
contour_radius = 2.0

LANES = 128
SUB = 8
REACH = ITERS
GROUP = 16
GRANT = 16 * 2**20
TABLES = 12
EDGE = 2


def contour(index):
    angle = math.pi * (index + 0.5) / POINTS
    return (
        contour_centre + contour_radius * math.cos(angle),
        contour_radius * math.sin(angle),
        contour_radius / POINTS * math.cos(angle),
        contour_radius / POINTS * math.sin(angle),
    )


def coefficients(pot, index):
    shift_real, shift_imag, weight_real, weight_imag = contour(index)
    offset = shift_real - (diag_shift + pot)
    scale = 1.0 / (offset * offset + shift_imag * shift_imag)
    real = offset * scale
    imag = -shift_imag * scale
    return (
        kinetic_half * real,
        kinetic_half * imag,
        weight_real * real - weight_imag * imag,
        weight_real * imag + weight_imag * real,
    )


def lane_ids():
    return lax.broadcasted_iota(jnp.int32, (SUB, LANES), 1)


def sub_ids():
    return lax.broadcasted_iota(jnp.int32, (SUB, LANES), 0)


def turn(value, shift):
    return pltpu.roll(value, shift % LANES, 1)


def spread(ref, row):
    return ref[pl.ds(row, SUB, stride=0), :]


def all_sublanes(value):
    for shift in (4, 2, 1):
        value = value + pltpu.roll(value, shift, 0)
    return value


def column_ids():
    return lane_ids() & (GROUP - 1)


def settle(packed):
    col = column_ids()
    low = (col >= REACH) & (col < 8)
    high = (col >= 8) & (col < GROUP - REACH)
    return jnp.where(low, packed, jnp.where(high, turn(packed, 10), 0.0))


def strip_of(tiles):
    lane = lane_ids()
    packed = jnp.zeros((SUB, LANES), jnp.float32)
    for z, value in enumerate(tiles):
        inside = ((lane + 2 - GROUP * z) & (LANES - 1)) < 10
        packed = jnp.where(inside, turn(value, GROUP * z + REACH), packed)
    return settle(packed)


def strip_of_layers(tile):
    moved = pltpu.roll(tile, REACH, 1, stride=GROUP, stride_axis=0)
    inside = ((lane_ids() + 2 - GROUP * sub_ids()) & (LANES - 1)) < 10
    return settle(all_sublanes(jnp.where(inside, moved, 0.0)))


def outer_lanes():
    col = column_ids()
    return (col < REACH) | (col >= GROUP - REACH)


def send_strip(strip):
    return jnp.where(column_ids() < 8, turn(strip, -10), turn(strip, 10))


def copy_rows(x_hbm, window, sems, height, cp):
    rows = x_hbm.shape[2]
    return [
        pltpu.make_async_copy(
            x_hbm.at[v, :, pl.ds(cp * (rows - height), height), :], window.at[:, v], sems.at[v]
        )
        for v in range(x_hbm.shape[0])
    ]


def pack_kernel(x_hbm, pot_hbm, out_ref, window, pot_buf, sems):
    cp = lax.axis_index("cp")
    vectors, nz, rows, _ = x_hbm.shape
    offset = cp * (rows - SUB)
    copies = copy_rows(x_hbm, window, sems, SUB, cp)
    copies.append(
        pltpu.make_async_copy(pot_hbm.at[:, pl.ds(offset, SUB), :], pot_buf, sems.at[vectors])
    )
    for copy in copies:
        copy.start()
    for copy in copies:
        copy.wait()
    flat = window.reshape(nz * vectors * SUB, LANES)
    pot = pot_buf.reshape(nz * SUB, LANES)
    for k in range(REACH):
        row = k + cp * (SUB - 1 - 2 * k)
        for z in range(nz):
            out_ref[k * nz + z] = flat[pl.ds(z * vectors * SUB + row, vectors, stride=SUB), :]
        out_ref[REACH * nz + k] = pot[pl.ds(row, nz, stride=SUB), :]


def add(total, value):
    return value if total is None else total + value


def fill_tables(tab, tile, slot):
    total = None
    sides = (tile, turn(tile, 1), turn(tile, -1))
    for j in range(POINTS):
        for d, side in enumerate(sides):
            values = coefficients(side, j)
            for q, value in enumerate(values):
                tab[slot(j * TABLES + 4 * d + q)] = value
            if d == 0:
                total = add(total, values[2])
    tab[slot(POINTS * TABLES)] = total


def first_step(coef, x, ub, r, nz):
    for z in range(nz):
        for j in range(POINTS):
            for q in range(2):
                ub[j, q, r, z] = coef(j, q, z) * x[z]


def cross(rows, z):
    above, here, below = rows
    near = above[z] + below[z]
    if z > 0:
        near = near + here[z - 1]
    if z + 1 < len(here):
        near = near + here[z + 1]
    return near


def second_step(coef, x, left, right, rows_of, store, nz):
    for j in range(POINTS):
        rows = [rows_of(j, q) for q in range(2)]
        for z in range(nz):
            near = [
                cross(rows[q], z)
                + (coef(j, 4 + q, z) * left[z] + coef(j, 8 + q, z) * right[z])
                for q in range(2)
            ]
            rest = x[z] - near[0]
            real, imag = coef(j, 0, z), coef(j, 1, z)
            store(j, 0, z, real * rest + imag * near[1])
            store(j, 1, z, imag * rest - real * near[1])


def third_step(coef, x, rows_of, nz):
    straight, ahead, back = [None] * nz, [None] * nz, [None] * nz
    for j in range(POINTS):
        rows = [rows_of(j, q) for q in range(2)]
        for z in range(nz):
            real, imag = rows[0][1][z], rows[1][1][z]
            straight[z] = add(
                straight[z],
                coef(j, 3, z) * cross(rows[1], z) - coef(j, 2, z) * cross(rows[0], z),
            )
            ahead[z] = add(ahead[z], coef(j, 11, z) * imag - coef(j, 10, z) * real)
            back[z] = add(back[z], coef(j, 7, z) * imag - coef(j, 6, z) * real)
    return [
        (coef(POINTS, 0, z) * x[z] + straight[z]) + (turn(ahead[z], 1) + turn(back[z], -1))
        for z in range(nz)
    ]


def interior_kernel(
    x_ref, pot_ref, part_ref, edge_ref, strip_ref, pot_strip_ref, window, xs, tab, ub, vb, sems
):
    cp = lax.axis_index("cp")
    vectors, nz, rows, _ = x_ref.shape
    height = window.shape[2]
    local = rows // 2 + REACH
    span = xs.shape[1]
    copies = copy_rows(x_ref, window, sems, height, cp)
    for copy in copies:
        copy.start()
    pot = pot_ref.reshape(nz * rows, LANES)
    table = tab.reshape((POINTS * TABLES + 1) * span * nz, LANES)
    for copy in copies:
        copy.wait()
    flat = window.reshape(nz * vectors * height, LANES)

    def coefs(r):
        def coef(j, q, z):
            return spread(table, ((j * TABLES + q) * span + r) * nz + z)

        return coef

    for r in range(local):
        tile = pot[pl.ds(r + cp * (rows - 1 - 2 * r), nz, stride=rows), :]
        fill_tables(tab, tile, lambda index: index * span + r)
        pot_strip_ref[r] = strip_of_layers(tile)
        tiles = []
        for z in range(nz):
            start = z * vectors * height + r + cp * (height - 1 - 2 * r)
            value = flat[pl.ds(start, vectors, stride=height), :]
            xs[0, r, z] = value
            xs[1, r, z] = turn(value, 1)
            xs[2, r, z] = turn(value, -1)
            tiles.append(value)
        strip_ref[r] = strip_of(tiles)

    def x_at(r, d=0):
        return [xs[d, r, z] for z in range(nz)]

    def around(ref, r):
        return lambda j, q: [[ref[j, q, r + d, z] for z in range(nz)] for d in (-1, 0, 1)]

    for r in range(local):
        first_step(coefs(r), x_at(r), ub, r, nz)

    def second(r, carry):
        def store(j, q, z, value):
            vb[j, q, r, z] = value

        second_step(coefs(r), x_at(r), x_at(r, 1), x_at(r, 2), around(ub, r), store, nz)
        return carry

    lax.fori_loop(1, local - 1, second, 0)
    for j in range(POINTS):
        for q in range(2):
            for r in range(1, REACH):
                for z in range(nz):
                    edge_ref[j, q, r - 1, z] = vb[j, q, r, z]

    def third(r, carry):
        for z, value in enumerate(third_step(coefs(r), x_at(r), around(vb, r), nz)):
            part_ref[r - 2, z] = value
        return carry

    lax.fori_loop(2, local - 2, third, 0)


def strip_kernel(recv_ref, strip_ref, pot_strip_ref, all_ref, pot_ref, send_ref):
    nz = recv_ref.shape[0] // REACH - 1
    local = strip_ref.shape[0]
    total = local + REACH
    pairs = total // 2
    sub = sub_ids()
    outer = outer_lanes()
    pots = [jnp.zeros((SUB, LANES), jnp.float32) for _ in range(pot_ref.shape[0])]
    sends = []
    for ri in range(total):
        if ri < REACH:
            k = REACH - 1 - ri
            strip = strip_of([recv_ref[k * nz + z] for z in range(nz)])
            pot = strip_of_layers(recv_ref[REACH * nz + k])
        else:
            strip = strip_ref[ri - REACH]
            pot = pot_strip_ref[ri - REACH]
        all_ref[ri] = strip
        sends.append(send_strip(strip))
        pots[ri // SUB] = jnp.where(sub == ri % SUB, pot, pots[ri // SUB])
    for ri in range(pairs):
        send_ref[ri] = jnp.where(outer, sends[ri], turn(sends[ri + pairs], 8))
    for t, value in enumerate(pots):
        pot_ref[t] = value
        send_ref[pairs + t] = send_strip(value)


def gram_sums(other_of, value, image, grams, images):
    for s in range(len(grams)):
        other = other_of if s == 0 else pltpu.roll(other_of, SUB - s, 0)
        grams[s] = add(grams[s], other * value)
        images[s] = add(images[s], other * image)


def border_kernel(
    own_ref, recv_ref, edge_ref, part_ref, pot_ref, out_ref, sums_ref, tab, xs, ub, vb
):
    cp = lax.axis_index("cp")
    nz, rows, _ = pot_ref.shape
    half = rows // 2
    span = REACH + 2
    table = tab.reshape((POINTS * TABLES + 1) * span * nz, LANES)

    def coefs(r):
        def coef(j, q, z):
            return spread(table, ((j * TABLES + q) * span + r + REACH) * nz + z)

        return coef

    def x_at(r):
        return [own_ref[r * nz + z] if r >= 0 else recv_ref[(-1 - r) * nz + z] for z in range(nz)]

    def around(ref, r):
        def one(j, q, row):
            if row >= 1 and ref is vb:
                return [edge_ref[j, q, row - 1, z] for z in range(nz)]
            return [ref[j, q, row + REACH, z] for z in range(nz)]

        return lambda j, q: [one(j, q, r + d) for d in (-1, 0, 1)]

    for r in range(-REACH, 2):
        tile = own_ref[REACH * nz + r] if r >= 0 else recv_ref[REACH * nz - 1 - r]
        fill_tables(tab, tile, lambda index: index * span + r + REACH)
    for r in range(-REACH, 2):
        first_step(coefs(r), x_at(r), ub, r + REACH, nz)
    for r in range(1 - REACH, 1):
        def store(j, q, z, value):
            vb[j, q, r + REACH, z] = value

        x = x_at(r)
        left = [turn(value, 1) for value in x]
        right = [turn(value, -1) for value in x]
        second_step(coefs(r), x, left, right, around(ub, r), store, nz)
    for r in range(-1, 2):
        for z, value in enumerate(third_step(coefs(r), x_at(r), around(vb, r), nz)):
            out_ref[r + 1, z] = value

    lane = lane_ids()
    kept = (lane >= EDGE) & (lane < LANES - EDGE)
    pot = pot_ref.reshape(nz * rows, LANES)
    count = SUB // 2 + 1
    grams, images = [None] * count, [None] * count

    def row_of(r):
        return [out_ref[r + 1, z] if r < 2 else part_ref[r - 2, z] for z in range(nz)]

    for r in range(half):
        row = r + cp * (rows - 1 - 2 * r)
        above, below = row_of(r - 1), row_of(r + 1)
        here = [jnp.where(kept, value, 0.0) for value in row_of(r)]
        for z in range(nz):
            value = here[z]
            near = cross((above, here, below), z) + (turn(value, 1) + turn(value, -1))
            image = (diag_shift + spread(pot, z * rows + row)) * value - kinetic_half * near
            gram_sums(value, value, image, grams, images)
    for s, value in enumerate(grams + images):
        sums_ref[s] = value


def close_kernel(
    all_ref, pot_strip_ref, recv_ref, border_ref, part_ref, sums_ref,
    own_ref, packet_ref, tab, xb, ub, vb, fb,
):
    cp = lax.axis_index("cp")
    nz, half = own_ref.shape[:2]
    total = all_ref.shape[0]
    pairs = total // 2
    tiles = pot_strip_ref.shape[0]
    lane = lane_ids()
    col = column_ids()
    outer = outer_lanes()
    lower = lane >= GROUP
    upper = lane < (nz - 1) * GROUP
    shifts = (0, 1, -1, GROUP, -GROUP)
    span = tiles * SUB

    for t in range(tiles):
        value = jnp.where(outer, recv_ref[pairs + t], pot_strip_ref[t])
        pot_strip = value
        tab[POINTS * 20 * tiles + t] = pot_strip
        for d, shift in enumerate(shifts):
            side = value if d == 0 else turn(value, shift)
            for j in range(POINTS):
                for q, item in enumerate(coefficients(side, j)):
                    tab[(j * 20 + d * 4 + q) * tiles + t] = item
    table = tab.reshape((POINTS * 20 + 1) * span, LANES)

    def coef(j, d, q, ri):
        return spread(table, (j * 20 + d * 4 + q) * span + ri)

    for ri in range(total):
        came = recv_ref[ri] if ri < pairs else turn(recv_ref[ri - pairs], -8)
        value = jnp.where(outer, came, all_ref[ri])
        xb[0, ri] = value
        if 1 <= ri < total - 1:
            xb[1, ri] = turn(value, 1)
            xb[2, ri] = turn(value, -1)
            xb[3, ri] = jnp.where(lower, turn(value, GROUP), 0.0)
            xb[4, ri] = jnp.where(upper, turn(value, -GROUP), 0.0)
        for j in range(POINTS):
            for q in range(2):
                ub[j, q, ri] = coef(j, 0, q, ri) * value

    for ri in range(1, total - 1):
        sides = [xb[d, ri] for d in range(5)]
        for j in range(POINTS):
            near = []
            for q in range(2):
                value = ub[j, q, ri - 1] + ub[j, q, ri + 1]
                for d in range(1, 5):
                    value = value + coef(j, d, q, ri) * sides[d]
                near.append(value)
            rest = sides[0] - near[0]
            real, imag = coef(j, 0, 0, ri), coef(j, 0, 1, ri)
            vb[j, 0, ri] = real * rest + imag * near[1]
            vb[j, 1, ri] = imag * rest - real * near[1]

    for ri in range(2, total - 2):
        parts = [None] * 5
        weight = None
        for j in range(POINTS):
            weight = add(weight, coef(j, 0, 2, ri))
            for d in range(5):
                if d == 0:
                    real, imag = [vb[j, q, ri - 1] + vb[j, q, ri + 1] for q in range(2)]
                else:
                    real, imag = vb[j, 0, ri], vb[j, 1, ri]
                parts[d] = add(parts[d], coef(j, d, 3, ri) * imag - coef(j, d, 2, ri) * real)
        value = weight * xb[0, ri] + parts[0]
        value = value + (turn(parts[1], -1) + turn(parts[2], 1))
        value = value + jnp.where(upper, turn(parts[3], -GROUP), 0.0)
        fb[ri] = value + jnp.where(lower, turn(parts[4], GROUP), 0.0)

    count = SUB // 2 + 1
    grams = [sums_ref[s] for s in range(count)]
    images = [sums_ref[count + s] for s in range(count)]
    whole = ((col >= REACH) & (col < REACH + EDGE)) | (
        (col >= GROUP - REACH - EDGE) & (col < GROUP - REACH)
    )
    edge = (lane < EDGE) | (lane >= LANES - EDGE)
    joined = (col >= GROUP - REACH) & (col < GROUP - REACH + EDGE)
    for r in range(half):
        ri = r + REACH
        value = fb[ri]
        left, right = turn(value, 1), turn(value, -1)
        near = (fb[ri - 1] + fb[ri + 1]) + (left + right)
        near = near + jnp.where(lower, turn(value, GROUP), 0.0)
        near = near + jnp.where(upper, turn(value, -GROUP), 0.0)
        pot = spread(table, POINTS * 20 * span + ri)
        image = (diag_shift + pot) * value - kinetic_half * near
        rest = jnp.where(
            col == REACH + EDGE, left, jnp.where(col == GROUP - REACH - EDGE - 1, right, 0.0)
        )
        image = jnp.where(whole, image, -kinetic_half * rest)
        gram_sums(value, jnp.where(whole, value, 0.0), image, grams, images)
        compact = jnp.where(joined, turn(value, 10), value)
        place = r + cp * (half - 1 - 2 * r)
        for z in range(nz):
            base = border_ref[r + 1, z] if r < 2 else part_ref[r - 2, z]
            moved = turn(compact, -EDGE - GROUP * z - (GROUP - REACH - EDGE))
            own_ref[z, place] = jnp.where(edge, moved, base)

    tile = jnp.zeros((SUB, LANES), jnp.float32)
    for s in range(count):
        tile = jnp.where(lane == s, jnp.sum(grams[s], axis=1, keepdims=True), tile)
        tile = jnp.where(lane == SUB + s, jnp.sum(images[s], axis=1, keepdims=True), tile)
    spun = pltpu.roll(tile, 0, 1, stride=GROUP, stride_axis=0)
    line = jnp.sum(spun, axis=0, keepdims=True)
    packet_ref[...] = jnp.broadcast_to(line[None], packet_ref.shape)


def factor_inverse(entry, size):
    work = [[entry(i, k) for k in range(i + 1)] for i in range(size)]
    root = []
    for k in range(size):
        root.append(lax.rsqrt(work[k][k]))
        for i in range(k + 1, size):
            work[i][k] = work[i][k] * root[k]
        for i in range(k + 1, size):
            for m in range(k + 1, i + 1):
                work[i][m] = work[i][m] - work[i][k] * work[m][k]
    inverse = [[None] * (i + 1) for i in range(size)]
    for i in range(size):
        inverse[i][i] = root[i]
        for k in range(i):
            total = None
            for m in range(k, i):
                total = add(total, work[i][m] * inverse[m][k])
            inverse[i][k] = -(total * root[i])
    return inverse


def finish_kernel(
    packet_ref, own_ref, other_ref, basis_hbm, projected_hbm, buf, out, small, sems, *, cells
):
    cp = lax.axis_index("cp")
    nz, half = own_ref.shape[:2]
    vectors = basis_hbm.shape[0]
    for z in range(nz):
        for r in range(half):
            buf[z, cp * half + r] = own_ref[z, r]
            buf[z, (1 - cp) * half + r] = other_ref[z, r]
    lane = lane_ids()
    sub = sub_ids()
    line = packet_ref[0:SUB, :]
    for start in range(SUB, packet_ref.shape[0], SUB):
        line = line + packet_ref[start : start + SUB, :]
    line = all_sublanes(line) * (1.0 / cells)

    def entry(i, k):
        s = (i - k) % SUB
        at = GROUP * k + s if s <= SUB // 2 else GROUP * i + SUB - s
        return jnp.broadcast_to(line[:, at : at + 1], (SUB, LANES))

    inverse = factor_inverse(entry, vectors)
    flat = buf.reshape(nz * 2 * half * vectors, LANES)
    copies = []
    for z in range(nz):
        for block in range(2 * half // SUB):
            loads = [
                flat[pl.ds((z * 2 * half + block * SUB) * vectors + b, SUB, stride=vectors), :]
                for b in range(vectors)
            ]
            for a in range(vectors):
                value = None
                for b in range(a + 1):
                    value = add(value, inverse[a][b] * loads[b])
                out[a, z, block * SUB : (block + 1) * SUB, :] = value
        copies.append(pltpu.make_async_copy(out.at[:, z], basis_hbm.at[:, z], sems.at[z]))
        copies[-1].start()

    tile = jnp.where((lane >> 4) == sub, line, 0.0)
    for shift in (4 * GROUP, 2 * GROUP, GROUP):
        tile = tile + turn(tile, shift)
    tile = turn(tile, -SUB)
    for s in range(SUB // 2 + 1, SUB):
        moved = turn(pltpu.roll(tile, SUB - s, 0), 2 * s - SUB)
        tile = jnp.where(lane == s, moved, tile)
    tile = jnp.where(lane < SUB, tile, 0.0)
    tile = tile + turn(tile, -SUB)
    image = jnp.where(lane < SUB, pltpu.roll(tile, 0, 1, stride=1, stride_axis=0), 0.0)
    whole = jnp.zeros((SUB, LANES), jnp.float32)
    mixed = None
    for b in range(vectors):
        column = jnp.zeros((SUB, LANES), jnp.float32)
        for a in range(b, vectors):
            column = jnp.where(sub == a, inverse[a][b], column)
        whole = jnp.where(lane == b, column, whole)
        mixed = add(mixed, column * image[b : b + 1, :])
    result = jnp.zeros((SUB, LANES), jnp.float32)
    for c in range(vectors):
        part = jnp.sum(mixed * whole[c : c + 1, :], axis=1, keepdims=True)
        result = jnp.where(lane == c, part, result)
    small[...] = result[:, :vectors]
    copies.append(pltpu.make_async_copy(small, projected_hbm, sems.at[nz]))
    copies[-1].start()
    for copy in copies:
        copy.wait()


def call(
    kernel, operands, outs, scratch, spaces, flops=0, out_spaces=None, grant=GRANT, **options
):
    return pl.pallas_call(
        functools.partial(kernel, **options),
        out_shape=[jax.ShapeDtypeStruct(shape, jnp.float32) for shape in outs],
        in_specs=[pl.BlockSpec(memory_space=space) for space in spaces],
        out_specs=[
            pl.BlockSpec(memory_space=space) for space in out_spaces or [pltpu.VMEM] * len(outs)
        ],
        scratch_shapes=scratch,
        compiler_params=pltpu.CompilerParams(vmem_limit_bytes=grant),
        cost_estimate=pl.CostEstimate(
            flops=flops,
            bytes_accessed=sum(value.size * 4 for value in operands)
            + sum(4 * math.prod(shape) for shape in outs),
            transcendentals=0,
        ),
    )(*operands)


def per_device(start_vectors, potential):
    vectors, nz, rows, columns = start_vectors.shape
    half = rows // 2
    local = half + REACH
    total = local + REACH
    height = -(-local // SUB) * SUB
    assert vectors == SUB and nz == SUB and columns == LANES
    assert lax.axis_size("cp") == 2 and rows % SUB == 0 and total % 2 == 0
    vmem, far, hbm = pltpu.VMEM, pl.ANY, pltpu.HBM
    tile = (SUB, LANES)

    def room(*shape):
        return pltpu.VMEM(shape + tile, jnp.float32)

    count = lax.axis_size("gy")
    swaps = []
    for g in range(count):
        swaps.append((2 * g, 2 * ((g - 1) % count) + 1))
        swaps.append((2 * g + 1, 2 * ((g + 1) % count)))
    (own_rows,) = call(
        pack_kernel,
        [pltpu.with_memory_space_constraint(value, hbm) for value in (start_vectors, potential)],
        [(REACH * (nz + 1),) + tile],
        [room(nz, vectors), room(nz), pltpu.SemaphoreType.DMA((vectors + 1,))],
        (hbm, hbm),
    )
    far_rows = lax.ppermute(own_rows, ("gy", "cp"), swaps)
    tables = POINTS * TABLES + 1
    part, edge, strip, pot_strip = call(
        interior_kernel, (start_vectors, potential),
        [(local - 4, nz) + tile, (POINTS, 2, REACH - 1, nz) + tile, (local,) + tile, (local,) + tile],
        [
            pltpu.VMEM((nz, vectors, height, LANES), jnp.float32),
            room(3, local + 2, nz),
            room(tables * (local + 2)),
            room(POINTS, 2, local + 2, nz),
            room(POINTS, 2, local, nz),
            pltpu.SemaphoreType.DMA((vectors,)),
        ],
        (far, vmem), flops=10**8,
    )
    tiles = -(-total // SUB)
    strips, pot_strips, send = call(
        strip_kernel, (far_rows, strip, pot_strip),
        [(total,) + tile, (tiles,) + tile, (total // 2 + tiles,) + tile],
        [], (vmem,) * 3,
    )
    size = lax.axis_size("gx")
    ahead = [(i, (i + 1) % size) for i in range(size)]
    back = [(i, (i - 1) % size) for i in range(size)]
    recv = lax.ppermute(send, "gx", ahead)
    if size > 2:
        other = lax.ppermute(send, "gx", back)
        recv = jnp.where((jnp.arange(LANES) % 8) < 4, recv, other)
    sums = 2 * (SUB // 2 + 1)
    border, partial = call(
        border_kernel, (own_rows, far_rows, edge, part, potential),
        [(REACH, nz) + tile, (sums,) + tile],
        [
            room(tables * (REACH + 2)),
            room(1),
            room(POINTS, 2, REACH + 2, nz),
            room(POINTS, 2, REACH + 2, nz),
        ],
        (vmem,) * 5, flops=3 * 10**7,
    )
    axes = ("gx", "gy", "cp")
    devices = math.prod(lax.axis_size(axis) for axis in axes)
    own, packet = call(
        close_kernel, (strips, pot_strips, recv, border, part, partial),
        [(nz, half) + tile, (devices, 1, LANES)],
        [
            room((POINTS * 20 + 1) * tiles),
            room(5, total),
            room(POINTS, 2, total),
            room(POINTS, 2, total),
            room(total),
        ],
        (vmem,) * 6, flops=10**7,
    )
    other = lax.ppermute(own, "cp", [(0, 1), (1, 0)])
    packets = lax.all_to_all(packet, axes, 0, 0, tiled=True).reshape(devices, LANES)
    cells = float(nz * rows * columns * lax.axis_size("gx") * lax.axis_size("gy"))
    basis, projected = call(
        finish_kernel, (packets, own, other),
        [(vectors, nz, rows, columns), (vectors, vectors)],
        [
            room(nz, rows),
            pltpu.VMEM((vectors, nz, rows, columns), jnp.float32),
            pltpu.VMEM((vectors, vectors), jnp.float32),
            pltpu.SemaphoreType.DMA((nz + 1,)),
        ],
        (vmem, vmem, vmem), out_spaces=(hbm, hbm), cells=cells,
    )
    return (basis, projected)


def solution(mesh):
    in_specs = (P(None, None, "gy", "gx"), P(None, "gy", "gx"))
    out_specs = (P(None, None, "gy", "gx"), P())
    return jax.shard_map(
        per_device, mesh=mesh, in_specs=in_specs, out_specs=out_specs, check_vma=False
    )
```

```python
import functools
import math

import jax
import jax.numpy as jnp
from jax import lax
from jax.experimental import pallas as pl
from jax.experimental.pallas import tpu as pltpu
from jax.sharding import PartitionSpec as P

POINTS = 4
ITERS = 3

diag_shift = 3.0
kinetic_half = 0.5
contour_centre = -1.0
contour_radius = 2.0

LANES = 128
SUB = 8
REACH = ITERS
GROUP = 16
GRANT = 16 * 2**20
TABLES = 12
EDGE = 2


def contour(index):
    angle = math.pi * (index + 0.5) / POINTS
    return (
        contour_centre + contour_radius * math.cos(angle),
        contour_radius * math.sin(angle),
        contour_radius / POINTS * math.cos(angle),
        contour_radius / POINTS * math.sin(angle),
    )


def coefficients(pot, index):
    shift_real, shift_imag, weight_real, weight_imag = contour(index)
    offset = shift_real - (diag_shift + pot)
    scale = 1.0 / (offset * offset + shift_imag * shift_imag)
    real = offset * scale
    imag = -shift_imag * scale
    return (
        kinetic_half * real,
        kinetic_half * imag,
        weight_real * real - weight_imag * imag,
        weight_real * imag + weight_imag * real,
    )


def lane_ids():
    return lax.broadcasted_iota(jnp.int32, (SUB, LANES), 1)


def sub_ids():
    return lax.broadcasted_iota(jnp.int32, (SUB, LANES), 0)


def turn(value, shift):
    return pltpu.roll(value, shift % LANES, 1)


def spread(ref, row):
    return ref[pl.ds(row, SUB, stride=0), :]


def all_sublanes(value):
    for shift in (4, 2, 1):
        value = value + pltpu.roll(value, shift, 0)
    return value


def column_ids():
    return lane_ids() & (GROUP - 1)


def settle(packed):
    col = column_ids()
    low = (col >= REACH) & (col < 8)
    high = (col >= 8) & (col < GROUP - REACH)
    return jnp.where(low, packed, jnp.where(high, turn(packed, 10), 0.0))


def strip_of(tiles):
    lane = lane_ids()
    packed = jnp.zeros((SUB, LANES), jnp.float32)
    for z, value in enumerate(tiles):
        inside = ((lane + 2 - GROUP * z) & (LANES - 1)) < 10
        packed = jnp.where(inside, turn(value, GROUP * z + REACH), packed)
    return settle(packed)


def strip_of_layers(tile):
    moved = pltpu.roll(tile, REACH, 1, stride=GROUP, stride_axis=0)
    inside = ((lane_ids() + 2 - GROUP * sub_ids()) & (LANES - 1)) < 10
    return settle(all_sublanes(jnp.where(inside, moved, 0.0)))


def outer_lanes():
    col = column_ids()
    return (col < REACH) | (col >= GROUP - REACH)


def send_strip(strip):
    return jnp.where(column_ids() < 8, turn(strip, -10), turn(strip, 10))


def copy_rows(x_hbm, window, sems, height, cp):
    rows = x_hbm.shape[2]
    return [
        pltpu.make_async_copy(
            x_hbm.at[v, :, pl.ds(cp * (rows - height), height), :], window.at[:, v], sems.at[v]
        )
        for v in range(x_hbm.shape[0])
    ]


def pack_kernel(x_hbm, pot_hbm, out_ref, window, pot_buf, sems):
    cp = lax.axis_index("cp")
    vectors, nz, rows, _ = x_hbm.shape
    copies = copy_rows(x_hbm, window, sems, SUB, 1 - cp)
    copies.append(
        pltpu.make_async_copy(
            pot_hbm.at[:, pl.ds((1 - cp) * (rows - SUB), SUB), :], pot_buf, sems.at[vectors]
        )
    )
    for copy in copies:
        copy.start()
    for copy in copies:
        copy.wait()
    flat = window.reshape(nz * vectors * SUB, LANES)
    pot = pot_buf.reshape(nz * SUB, LANES)
    for k in range(REACH):
        row = k + (1 - cp) * (SUB - 1 - 2 * k)
        for z in range(nz):
            out_ref[k * nz + z] = flat[pl.ds(z * vectors * SUB + row, vectors, stride=SUB), :]
        out_ref[REACH * nz + k] = pot[pl.ds(row, nz, stride=SUB), :]


def add(total, value):
    return value if total is None else total + value


def fill_tables(tab, tile, slot):
    total = None
    sides = (tile, turn(tile, 1), turn(tile, -1))
    for j in range(POINTS):
        for d, side in enumerate(sides):
            values = coefficients(side, j)
            for q, value in enumerate(values):
                tab[slot(j * TABLES + 4 * d + q)] = value
            if d == 0:
                total = add(total, values[2])
    tab[slot(POINTS * TABLES)] = total


def first_step(coef, x, ub, r, nz):
    for z in range(nz):
        for j in range(POINTS):
            for q in range(2):
                ub[j, q, r, z] = coef(j, q, z) * x[z]


def cross(rows, z):
    above, here, below = rows
    near = above[z] + below[z]
    if z > 0:
        near = near + here[z - 1]
    if z + 1 < len(here):
        near = near + here[z + 1]
    return near


def second_step(coef, x, left, right, rows_of, store, nz):
    for j in range(POINTS):
        rows = [rows_of(j, q) for q in range(2)]
        for z in range(nz):
            near = [
                cross(rows[q], z)
                + (coef(j, 4 + q, z) * left[z] + coef(j, 8 + q, z) * right[z])
                for q in range(2)
            ]
            rest = x[z] - near[0]
            real, imag = coef(j, 0, z), coef(j, 1, z)
            store(j, 0, z, real * rest + imag * near[1])
            store(j, 1, z, imag * rest - real * near[1])


def third_step(coef, x, rows_of, nz):
    straight, ahead, back = [None] * nz, [None] * nz, [None] * nz
    for j in range(POINTS):
        rows = [rows_of(j, q) for q in range(2)]
        for z in range(nz):
            real, imag = rows[0][1][z], rows[1][1][z]
            straight[z] = add(
                straight[z],
                coef(j, 3, z) * cross(rows[1], z) - coef(j, 2, z) * cross(rows[0], z),
            )
            ahead[z] = add(ahead[z], coef(j, 11, z) * imag - coef(j, 10, z) * real)
            back[z] = add(back[z], coef(j, 7, z) * imag - coef(j, 6, z) * real)
    return [
        (coef(POINTS, 0, z) * x[z] + straight[z]) + (turn(ahead[z], 1) + turn(back[z], -1))
        for z in range(nz)
    ]


def interior_kernel(
    x_ref, pot_ref, part_ref, edge_ref, strip_ref, pot_strip_ref, own_ref,
    window, xs, tab, ub, vb, sems,
):
    cp = lax.axis_index("cp")
    vectors, nz, rows, _ = x_ref.shape
    height = window.shape[2]
    local = rows // 2 + REACH
    span = xs.shape[1]
    copies = copy_rows(x_ref, window, sems, height, cp)
    for copy in copies:
        copy.start()
    pot = pot_ref.reshape(nz * rows, LANES)
    table = tab.reshape((POINTS * TABLES + 1) * span * nz, LANES)
    for copy in copies:
        copy.wait()
    flat = window.reshape(nz * vectors * height, LANES)

    def coefs(r):
        def coef(j, q, z):
            return spread(table, ((j * TABLES + q) * span + r) * nz + z)

        return coef

    for r in range(local):
        tile = pot[pl.ds(r + cp * (rows - 1 - 2 * r), nz, stride=rows), :]
        fill_tables(tab, tile, lambda index: index * span + r)
        pot_strip_ref[r] = strip_of_layers(tile)
        tiles = []
        for z in range(nz):
            start = z * vectors * height + r + cp * (height - 1 - 2 * r)
            value = flat[pl.ds(start, vectors, stride=height), :]
            xs[0, r, z] = value
            xs[1, r, z] = turn(value, 1)
            xs[2, r, z] = turn(value, -1)
            tiles.append(value)
            if r < REACH - 1:
                own_ref[r * nz + z] = value
        if r < REACH - 1:
            own_ref[(REACH - 1) * nz + r] = tile
        strip_ref[r] = strip_of(tiles)

    def x_at(r, d=0):
        return [xs[d, r, z] for z in range(nz)]

    def around(ref, r):
        return lambda j, q: [[ref[j, q, r + d, z] for z in range(nz)] for d in (-1, 0, 1)]

    for r in range(local):
        first_step(coefs(r), x_at(r), ub, r, nz)

    def second(r, carry):
        def store(j, q, z, value):
            vb[j, q, r, z] = value

        second_step(coefs(r), x_at(r), x_at(r, 1), x_at(r, 2), around(ub, r), store, nz)
        return carry

    lax.fori_loop(1, local - 1, second, 0)
    for j in range(POINTS):
        for q in range(2):
            for r in range(1, REACH):
                for z in range(nz):
                    edge_ref[j, q, r - 1, z] = vb[j, q, r, z]

    def third(r, carry):
        for z, value in enumerate(third_step(coefs(r), x_at(r), around(vb, r), nz)):
            part_ref[r - 2, z] = value
        return carry

    lax.fori_loop(2, local - 2, third, 0)


def strip_kernel(recv_ref, strip_ref, pot_strip_ref, all_ref, pot_ref, send_ref):
    nz = recv_ref.shape[0] // REACH - 1
    local = strip_ref.shape[0]
    total = local + REACH
    pairs = total // 2
    sub = sub_ids()
    outer = outer_lanes()
    pots = [jnp.zeros((SUB, LANES), jnp.float32) for _ in range(pot_ref.shape[0])]
    sends = []
    for ri in range(total):
        if ri < REACH:
            k = REACH - 1 - ri
            strip = strip_of([recv_ref[k * nz + z] for z in range(nz)])
            pot = strip_of_layers(recv_ref[REACH * nz + k])
        else:
            strip = strip_ref[ri - REACH]
            pot = pot_strip_ref[ri - REACH]
        all_ref[ri] = strip
        sends.append(send_strip(strip))
        pots[ri // SUB] = jnp.where(sub == ri % SUB, pot, pots[ri // SUB])
    for ri in range(pairs):
        send_ref[ri] = jnp.where(outer, sends[ri], turn(sends[ri + pairs], 8))
    for t, value in enumerate(pots):
        pot_ref[t] = value
        send_ref[pairs + t] = send_strip(value)


def gram_sums(other_of, value, image, grams, images):
    for s in range(len(grams)):
        other = other_of if s == 0 else pltpu.roll(other_of, SUB - s, 0)
        grams[s] = add(grams[s], other * value)
        images[s] = add(images[s], other * image)


def border_kernel(
    own_ref, recv_ref, edge_ref, part_ref, pot_ref, out_ref, sums_ref, tab, xs, ub, vb
):
    cp = lax.axis_index("cp")
    nz, rows, _ = pot_ref.shape
    half = rows // 2
    span = REACH + 2
    table = tab.reshape((POINTS * TABLES + 1) * span * nz, LANES)

    def coefs(r):
        def coef(j, q, z):
            return spread(table, ((j * TABLES + q) * span + r + REACH) * nz + z)

        return coef

    def x_at(r):
        return [own_ref[r * nz + z] if r >= 0 else recv_ref[(-1 - r) * nz + z] for z in range(nz)]

    def around(ref, r):
        def one(j, q, row):
            if row >= 1 and ref is vb:
                return [edge_ref[j, q, row - 1, z] for z in range(nz)]
            return [ref[j, q, row + REACH, z] for z in range(nz)]

        return lambda j, q: [one(j, q, r + d) for d in (-1, 0, 1)]

    for r in range(-REACH, 2):
        tile = own_ref[(REACH - 1) * nz + r] if r >= 0 else recv_ref[REACH * nz - 1 - r]
        fill_tables(tab, tile, lambda index: index * span + r + REACH)
    for r in range(-REACH, 2):
        first_step(coefs(r), x_at(r), ub, r + REACH, nz)
    for r in range(1 - REACH, 1):
        def store(j, q, z, value):
            vb[j, q, r + REACH, z] = value

        x = x_at(r)
        left = [turn(value, 1) for value in x]
        right = [turn(value, -1) for value in x]
        second_step(coefs(r), x, left, right, around(ub, r), store, nz)
    for r in range(-1, 2):
        for z, value in enumerate(third_step(coefs(r), x_at(r), around(vb, r), nz)):
            out_ref[r + 1, z] = value

    lane = lane_ids()
    kept = (lane >= EDGE) & (lane < LANES - EDGE)
    pot = pot_ref.reshape(nz * rows, LANES)
    count = SUB // 2 + 1
    grams, images = [None] * count, [None] * count

    def row_of(r):
        return [out_ref[r + 1, z] if r < 2 else part_ref[r - 2, z] for z in range(nz)]

    for r in range(half):
        row = r + cp * (rows - 1 - 2 * r)
        above, below = row_of(r - 1), row_of(r + 1)
        here = [jnp.where(kept, value, 0.0) for value in row_of(r)]
        for z in range(nz):
            value = here[z]
            near = cross((above, here, below), z) + (turn(value, 1) + turn(value, -1))
            image = (diag_shift + spread(pot, z * rows + row)) * value - kinetic_half * near
            gram_sums(value, value, image, grams, images)
    for s, value in enumerate(grams + images):
        sums_ref[s] = value


def close_kernel(
    all_ref, pot_strip_ref, recv_ref, border_ref, part_ref, sums_ref,
    own_ref, packet_ref, tab, xb, ub, vb, fb,
):
    cp = lax.axis_index("cp")
    nz, half = own_ref.shape[:2]
    total = all_ref.shape[0]
    pairs = total // 2
    tiles = pot_strip_ref.shape[0]
    lane = lane_ids()
    col = column_ids()
    outer = outer_lanes()
    lower = lane >= GROUP
    upper = lane < (nz - 1) * GROUP
    shifts = (0, 1, -1, GROUP, -GROUP)
    span = tiles * SUB

    for t in range(tiles):
        value = jnp.where(outer, recv_ref[pairs + t], pot_strip_ref[t])
        pot_strip = value
        tab[POINTS * 20 * tiles + t] = pot_strip
        for d, shift in enumerate(shifts):
            side = value if d == 0 else turn(value, shift)
            for j in range(POINTS):
                for q, item in enumerate(coefficients(side, j)):
                    tab[(j * 20 + d * 4 + q) * tiles + t] = item
    table = tab.reshape((POINTS * 20 + 1) * span, LANES)

    def coef(j, d, q, ri):
        return spread(table, (j * 20 + d * 4 + q) * span + ri)

    for ri in range(total):
        came = recv_ref[ri] if ri < pairs else turn(recv_ref[ri - pairs], -8)
        value = jnp.where(outer, came, all_ref[ri])
        xb[0, ri] = value
        if 1 <= ri < total - 1:
            xb[1, ri] = turn(value, 1)
            xb[2, ri] = turn(value, -1)
            xb[3, ri] = jnp.where(lower, turn(value, GROUP), 0.0)
            xb[4, ri] = jnp.where(upper, turn(value, -GROUP), 0.0)
        for j in range(POINTS):
            for q in range(2):
                ub[j, q, ri] = coef(j, 0, q, ri) * value

    for ri in range(1, total - 1):
        sides = [xb[d, ri] for d in range(5)]
        for j in range(POINTS):
            near = []
            for q in range(2):
                value = ub[j, q, ri - 1] + ub[j, q, ri + 1]
                for d in range(1, 5):
                    value = value + coef(j, d, q, ri) * sides[d]
                near.append(value)
            rest = sides[0] - near[0]
            real, imag = coef(j, 0, 0, ri), coef(j, 0, 1, ri)
            vb[j, 0, ri] = real * rest + imag * near[1]
            vb[j, 1, ri] = imag * rest - real * near[1]

    for ri in range(2, total - 2):
        parts = [None] * 5
        weight = None
        for j in range(POINTS):
            weight = add(weight, coef(j, 0, 2, ri))
            for d in range(5):
                if d == 0:
                    real, imag = [vb[j, q, ri - 1] + vb[j, q, ri + 1] for q in range(2)]
                else:
                    real, imag = vb[j, 0, ri], vb[j, 1, ri]
                parts[d] = add(parts[d], coef(j, d, 3, ri) * imag - coef(j, d, 2, ri) * real)
        value = weight * xb[0, ri] + parts[0]
        value = value + (turn(parts[1], -1) + turn(parts[2], 1))
        value = value + jnp.where(upper, turn(parts[3], -GROUP), 0.0)
        fb[ri] = value + jnp.where(lower, turn(parts[4], GROUP), 0.0)

    count = SUB // 2 + 1
    grams = [sums_ref[s] for s in range(count)]
    images = [sums_ref[count + s] for s in range(count)]
    whole = ((col >= REACH) & (col < REACH + EDGE)) | (
        (col >= GROUP - REACH - EDGE) & (col < GROUP - REACH)
    )
    edge = (lane < EDGE) | (lane >= LANES - EDGE)
    joined = (col >= GROUP - REACH) & (col < GROUP - REACH + EDGE)
    for r in range(half):
        ri = r + REACH
        value = fb[ri]
        left, right = turn(value, 1), turn(value, -1)
        near = (fb[ri - 1] + fb[ri + 1]) + (left + right)
        near = near + jnp.where(lower, turn(value, GROUP), 0.0)
        near = near + jnp.where(upper, turn(value, -GROUP), 0.0)
        pot = spread(table, POINTS * 20 * span + ri)
        image = (diag_shift + pot) * value - kinetic_half * near
        rest = jnp.where(
            col == REACH + EDGE, left, jnp.where(col == GROUP - REACH - EDGE - 1, right, 0.0)
        )
        image = jnp.where(whole, image, -kinetic_half * rest)
        gram_sums(value, jnp.where(whole, value, 0.0), image, grams, images)
        compact = jnp.where(joined, turn(value, 10), value)
        place = r + cp * (half - 1 - 2 * r)
        for z in range(nz):
            base = border_ref[r + 1, z] if r < 2 else part_ref[r - 2, z]
            moved = turn(compact, -EDGE - GROUP * z - (GROUP - REACH - EDGE))
            own_ref[z, place] = jnp.where(edge, moved, base)

    tile = jnp.zeros((SUB, LANES), jnp.float32)
    for s in range(count):
        tile = jnp.where(lane == s, jnp.sum(grams[s], axis=1, keepdims=True), tile)
        tile = jnp.where(lane == SUB + s, jnp.sum(images[s], axis=1, keepdims=True), tile)
    spun = pltpu.roll(tile, 0, 1, stride=GROUP, stride_axis=0)
    line = jnp.sum(spun, axis=0, keepdims=True)
    packet_ref[...] = jnp.broadcast_to(line[None], packet_ref.shape)


def factor_inverse(entry, size):
    work = [[entry(i, k) for k in range(i + 1)] for i in range(size)]
    root = []
    for k in range(size):
        root.append(lax.rsqrt(work[k][k]))
        for i in range(k + 1, size):
            work[i][k] = work[i][k] * root[k]
        for i in range(k + 1, size):
            for m in range(k + 1, i + 1):
                work[i][m] = work[i][m] - work[i][k] * work[m][k]
    inverse = [[None] * (i + 1) for i in range(size)]
    for i in range(size):
        inverse[i][i] = root[i]
        for k in range(i):
            total = None
            for m in range(k, i):
                total = add(total, work[i][m] * inverse[m][k])
            inverse[i][k] = -(total * root[i])
    return inverse


def finish_kernel(
    packet_ref, own_ref, other_ref, basis_hbm, projected_hbm, buf, out, small, sems, *, cells
):
    cp = lax.axis_index("cp")
    nz, half = own_ref.shape[:2]
    vectors = basis_hbm.shape[0]
    for z in range(nz):
        for r in range(half):
            buf[z, cp * half + r] = own_ref[z, r]
            buf[z, (1 - cp) * half + r] = other_ref[z, r]
    lane = lane_ids()
    sub = sub_ids()
    line = packet_ref[0:SUB, :]
    for start in range(SUB, packet_ref.shape[0], SUB):
        line = line + packet_ref[start : start + SUB, :]
    line = all_sublanes(line) * (1.0 / cells)

    def entry(i, k):
        s = (i - k) % SUB
        at = GROUP * k + s if s <= SUB // 2 else GROUP * i + SUB - s
        return jnp.broadcast_to(line[:, at : at + 1], (SUB, LANES))

    inverse = factor_inverse(entry, vectors)
    flat = buf.reshape(nz * 2 * half * vectors, LANES)
    copies = []
    for z in range(nz):
        for block in range(2 * half // SUB):
            loads = [
                flat[pl.ds((z * 2 * half + block * SUB) * vectors + b, SUB, stride=vectors), :]
                for b in range(vectors)
            ]
            for a in range(vectors):
                value = None
                for b in range(a + 1):
                    value = add(value, inverse[a][b] * loads[b])
                out[a, z, block * SUB : (block + 1) * SUB, :] = value
        copies.append(pltpu.make_async_copy(out.at[:, z], basis_hbm.at[:, z], sems.at[z]))
        copies[-1].start()

    tile = jnp.where((lane >> 4) == sub, line, 0.0)
    for shift in (4 * GROUP, 2 * GROUP, GROUP):
        tile = tile + turn(tile, shift)
    tile = turn(tile, -SUB)
    for s in range(SUB // 2 + 1, SUB):
        moved = turn(pltpu.roll(tile, SUB - s, 0), 2 * s - SUB)
        tile = jnp.where(lane == s, moved, tile)
    tile = jnp.where(lane < SUB, tile, 0.0)
    tile = tile + turn(tile, -SUB)
    image = jnp.where(lane < SUB, pltpu.roll(tile, 0, 1, stride=1, stride_axis=0), 0.0)
    whole = jnp.zeros((SUB, LANES), jnp.float32)
    mixed = None
    for b in range(vectors):
        column = jnp.zeros((SUB, LANES), jnp.float32)
        for a in range(b, vectors):
            column = jnp.where(sub == a, inverse[a][b], column)
        whole = jnp.where(lane == b, column, whole)
        mixed = add(mixed, column * image[b : b + 1, :])
    result = jnp.zeros((SUB, LANES), jnp.float32)
    for c in range(vectors):
        part = jnp.sum(mixed * whole[c : c + 1, :], axis=1, keepdims=True)
        result = jnp.where(lane == c, part, result)
    small[...] = result[:, :vectors]
    copies.append(pltpu.make_async_copy(small, projected_hbm, sems.at[nz]))
    copies[-1].start()
    for copy in copies:
        copy.wait()


def call(
    kernel, operands, outs, scratch, spaces, flops=0, out_spaces=None, grant=GRANT, **options
):
    return pl.pallas_call(
        functools.partial(kernel, **options),
        out_shape=[jax.ShapeDtypeStruct(shape, jnp.float32) for shape in outs],
        in_specs=[pl.BlockSpec(memory_space=space) for space in spaces],
        out_specs=[
            pl.BlockSpec(memory_space=space) for space in out_spaces or [pltpu.VMEM] * len(outs)
        ],
        scratch_shapes=scratch,
        compiler_params=pltpu.CompilerParams(vmem_limit_bytes=grant),
        cost_estimate=pl.CostEstimate(
            flops=flops,
            bytes_accessed=sum(value.size * 4 for value in operands)
            + sum(4 * math.prod(shape) for shape in outs),
            transcendentals=0,
        ),
    )(*operands)


def per_device(start_vectors, potential):
    vectors, nz, rows, columns = start_vectors.shape
    half = rows // 2
    local = half + REACH
    total = local + REACH
    height = -(-local // SUB) * SUB
    assert vectors == SUB and nz == SUB and columns == LANES
    assert lax.axis_size("cp") == 2 and rows % SUB == 0 and total % 2 == 0
    vmem, far, hbm = pltpu.VMEM, pl.ANY, pltpu.HBM
    tile = (SUB, LANES)

    def room(*shape):
        return pltpu.VMEM(shape + tile, jnp.float32)

    count = lax.axis_size("gy")
    rings = []
    for g in range(count):
        rings.append((2 * g, 2 * ((g + 1) % count)))
        rings.append((2 * g + 1, 2 * ((g - 1) % count) + 1))
    (rows_out,) = call(
        pack_kernel,
        [pltpu.with_memory_space_constraint(value, hbm) for value in (start_vectors, potential)],
        [(REACH * (nz + 1),) + tile],
        [room(nz, vectors), room(nz), pltpu.SemaphoreType.DMA((vectors + 1,))],
        (hbm, hbm),
    )
    far_rows = lax.ppermute(rows_out, ("gy", "cp"), rings)
    tables = POINTS * TABLES + 1
    part, edge, strip, pot_strip, own_rows = call(
        interior_kernel, (start_vectors, potential),
        [(local - 4, nz) + tile, (POINTS, 2, REACH - 1, nz) + tile]
        + [(local,) + tile] * 2 + [((REACH - 1) * (nz + 1),) + tile],
        [
            pltpu.VMEM((nz, vectors, height, LANES), jnp.float32),
            room(3, local + 2, nz),
            room(tables * (local + 2)),
            room(POINTS, 2, local + 2, nz),
            room(POINTS, 2, local, nz),
            pltpu.SemaphoreType.DMA((vectors,)),
        ],
        (far, vmem), flops=10**8,
    )
    tiles = -(-total // SUB)
    strips, pot_strips, send = call(
        strip_kernel, (far_rows, strip, pot_strip),
        [(total,) + tile, (tiles,) + tile, (total // 2 + tiles,) + tile],
        [], (vmem,) * 3,
    )
    size = lax.axis_size("gx")
    ahead = [(i, (i + 1) % size) for i in range(size)]
    back = [(i, (i - 1) % size) for i in range(size)]
    recv = lax.ppermute(send, "gx", ahead)
    if size > 2:
        other = lax.ppermute(send, "gx", back)
        recv = jnp.where((jnp.arange(LANES) % 8) < 4, recv, other)
    sums = 2 * (SUB // 2 + 1)
    border, partial = call(
        border_kernel, (own_rows, far_rows, edge, part, potential),
        [(REACH, nz) + tile, (sums,) + tile],
        [
            room(tables * (REACH + 2)),
            room(1),
            room(POINTS, 2, REACH + 2, nz),
            room(POINTS, 2, REACH + 2, nz),
        ],
        (vmem,) * 5, flops=3 * 10**7,
    )
    axes = ("gx", "gy", "cp")
    devices = math.prod(lax.axis_size(axis) for axis in axes)
    own, packet = call(
        close_kernel, (strips, pot_strips, recv, border, part, partial),
        [(nz, half) + tile, (devices, 1, LANES)],
        [
            room((POINTS * 20 + 1) * tiles),
            room(5, total),
            room(POINTS, 2, total),
            room(POINTS, 2, total),
            room(total),
        ],
        (vmem,) * 6, flops=10**7,
    )
    other = lax.ppermute(own, "cp", [(0, 1), (1, 0)])
    packets = lax.all_to_all(packet, axes, 0, 0, tiled=True).reshape(devices, LANES)
    cells = float(nz * rows * columns * lax.axis_size("gx") * lax.axis_size("gy"))
    basis, projected = call(
        finish_kernel, (packets, own, other),
        [(vectors, nz, rows, columns), (vectors, vectors)],
        [
            room(nz, rows),
            pltpu.VMEM((vectors, nz, rows, columns), jnp.float32),
            pltpu.VMEM((vectors, vectors), jnp.float32),
            pltpu.SemaphoreType.DMA((nz + 1,)),
        ],
        (vmem, vmem, vmem), out_spaces=(hbm, hbm), cells=cells,
    )
    return (basis, projected)


def solution(mesh):
    in_specs = (P(None, None, "gy", "gx"), P(None, "gy", "gx"))
    out_specs = (P(None, None, "gy", "gx"), P())
    return jax.shard_map(
        per_device, mesh=mesh, in_specs=in_specs, out_specs=out_specs, check_vma=False
    )
```

```python
import functools
import math

import jax
import jax.numpy as jnp
from jax import lax
from jax.experimental import pallas as pl
from jax.experimental.pallas import tpu as pltpu
from jax.sharding import PartitionSpec as P

POINTS = 4
ITERS = 3

diag_shift = 3.0
kinetic_half = 0.5
contour_centre = -1.0
contour_radius = 2.0

LANES = 128
SUB = 8
REACH = ITERS
GROUP = 16
GRANT = 16 * 2**20
TABLES = 12
EDGE = 2


def contour(index):
    angle = math.pi * (index + 0.5) / POINTS
    return (
        contour_centre + contour_radius * math.cos(angle),
        contour_radius * math.sin(angle),
        contour_radius / POINTS * math.cos(angle),
        contour_radius / POINTS * math.sin(angle),
    )


def coefficients(pot, index):
    shift_real, shift_imag, weight_real, weight_imag = contour(index)
    offset = shift_real - (diag_shift + pot)
    scale = 1.0 / (offset * offset + shift_imag * shift_imag)
    real = offset * scale
    imag = -shift_imag * scale
    return (
        kinetic_half * real,
        kinetic_half * imag,
        weight_real * real - weight_imag * imag,
        weight_real * imag + weight_imag * real,
    )


def lane_ids():
    return lax.broadcasted_iota(jnp.int32, (SUB, LANES), 1)


def sub_ids():
    return lax.broadcasted_iota(jnp.int32, (SUB, LANES), 0)


def turn(value, shift):
    return pltpu.roll(value, shift % LANES, 1)


def spread(ref, row):
    return ref[pl.ds(row, SUB, stride=0), :]


def all_sublanes(value):
    for shift in (4, 2, 1):
        value = value + pltpu.roll(value, shift, 0)
    return value


def column_ids():
    return lane_ids() & (GROUP - 1)


def settle(packed):
    col = column_ids()
    low = (col >= REACH) & (col < 8)
    high = (col >= 8) & (col < GROUP - REACH)
    return jnp.where(low, packed, jnp.where(high, turn(packed, 10), 0.0))


def strip_of(tiles):
    lane = lane_ids()
    packed = jnp.zeros((SUB, LANES), jnp.float32)
    for z, value in enumerate(tiles):
        inside = ((lane + 2 - GROUP * z) & (LANES - 1)) < 10
        packed = jnp.where(inside, turn(value, GROUP * z + REACH), packed)
    return settle(packed)


def strip_of_layers(tile):
    moved = pltpu.roll(tile, REACH, 1, stride=GROUP, stride_axis=0)
    inside = ((lane_ids() + 2 - GROUP * sub_ids()) & (LANES - 1)) < 10
    return settle(all_sublanes(jnp.where(inside, moved, 0.0)))


def outer_lanes():
    col = column_ids()
    return (col < REACH) | (col >= GROUP - REACH)


def send_strip(strip):
    return jnp.where(column_ids() < 8, turn(strip, -10), turn(strip, 10))


def copy_rows(x_hbm, window, sems, height, cp):
    rows = x_hbm.shape[2]
    return [
        pltpu.make_async_copy(
            x_hbm.at[v, :, pl.ds(cp * (rows - height), height), :], window.at[:, v], sems.at[v]
        )
        for v in range(x_hbm.shape[0])
    ]


def pack_kernel(x_hbm, pot_hbm, out_ref, window, pot_buf, sems):
    cp = lax.axis_index("cp")
    vectors, nz, rows, _ = x_hbm.shape
    copies = copy_rows(x_hbm, window, sems, SUB, 1 - cp)
    copies.append(
        pltpu.make_async_copy(
            pot_hbm.at[:, pl.ds((1 - cp) * (rows - SUB), SUB), :], pot_buf, sems.at[vectors]
        )
    )
    for copy in copies:
        copy.start()
    for copy in copies:
        copy.wait()
    flat = window.reshape(nz * vectors * SUB, LANES)
    pot = pot_buf.reshape(nz * SUB, LANES)
    for k in range(REACH):
        row = k + (1 - cp) * (SUB - 1 - 2 * k)
        for z in range(nz):
            out_ref[k * nz + z] = flat[pl.ds(z * vectors * SUB + row, vectors, stride=SUB), :]
        out_ref[REACH * nz + k] = pot[pl.ds(row, nz, stride=SUB), :]


def add(total, value):
    return value if total is None else total + value


def fill_tables(tab, tile, slot, steps=3):
    total = None
    sides = (tile, turn(tile, 1), turn(tile, -1))
    for j in range(POINTS):
        for d, side in enumerate(sides if steps > 1 else sides[:1]):
            values = coefficients(side, j)
            for q, value in enumerate(values if steps > 2 else values[:2]):
                tab[slot(j * TABLES + 4 * d + q)] = value
            if d == 0:
                total = add(total, values[2])
    if steps > 2:
        tab[slot(POINTS * TABLES)] = total


def first_step(coef, x, ub, r, nz):
    for z in range(nz):
        for j in range(POINTS):
            for q in range(2):
                ub[j, q, r, z] = coef(j, q, z) * x[z]


def cross(rows, z):
    above, here, below = rows
    near = above[z] + below[z]
    if z > 0:
        near = near + here[z - 1]
    if z + 1 < len(here):
        near = near + here[z + 1]
    return near


def second_step(coef, x, left, right, rows_of, store, nz):
    for j in range(POINTS):
        rows = [rows_of(j, q) for q in range(2)]
        for z in range(nz):
            near = [
                cross(rows[q], z)
                + (coef(j, 4 + q, z) * left[z] + coef(j, 8 + q, z) * right[z])
                for q in range(2)
            ]
            rest = x[z] - near[0]
            real, imag = coef(j, 0, z), coef(j, 1, z)
            store(j, 0, z, real * rest + imag * near[1])
            store(j, 1, z, imag * rest - real * near[1])


def third_step(coef, x, rows_of, nz):
    straight, ahead, back = [None] * nz, [None] * nz, [None] * nz
    for j in range(POINTS):
        rows = [rows_of(j, q) for q in range(2)]
        for z in range(nz):
            real, imag = rows[0][1][z], rows[1][1][z]
            straight[z] = add(
                straight[z],
                coef(j, 3, z) * cross(rows[1], z) - coef(j, 2, z) * cross(rows[0], z),
            )
            ahead[z] = add(ahead[z], coef(j, 11, z) * imag - coef(j, 10, z) * real)
            back[z] = add(back[z], coef(j, 7, z) * imag - coef(j, 6, z) * real)
    return [
        (coef(POINTS, 0, z) * x[z] + straight[z]) + (turn(ahead[z], 1) + turn(back[z], -1))
        for z in range(nz)
    ]


def interior_kernel(
    x_ref, pot_ref, part_ref, edge_ref, strip_ref, pot_strip_ref, own_ref,
    window, xs, tab, ub, vb, sems,
):
    cp = lax.axis_index("cp")
    vectors, nz, rows, _ = x_ref.shape
    height = window.shape[2]
    local = rows // 2 + REACH
    span = xs.shape[1]
    copies = copy_rows(x_ref, window, sems, height, cp)
    for copy in copies:
        copy.start()
    pot = pot_ref.reshape(nz * rows, LANES)
    table = tab.reshape((POINTS * TABLES + 1) * span * nz, LANES)
    for copy in copies:
        copy.wait()
    flat = window.reshape(nz * vectors * height, LANES)

    def coefs(r):
        def coef(j, q, z):
            return spread(table, ((j * TABLES + q) * span + r) * nz + z)

        return coef

    for r in range(local):
        tile = pot[pl.ds(r + cp * (rows - 1 - 2 * r), nz, stride=rows), :]
        fill_tables(tab, tile, lambda index: index * span + r, 1 + min(r, local - 1 - r, 2))
        pot_strip_ref[r] = strip_of_layers(tile)
        tiles = []
        for z in range(nz):
            start = z * vectors * height + r + cp * (height - 1 - 2 * r)
            value = flat[pl.ds(start, vectors, stride=height), :]
            xs[0, r, z] = value
            xs[1, r, z] = turn(value, 1)
            xs[2, r, z] = turn(value, -1)
            tiles.append(value)
            if r < REACH - 1:
                own_ref[r * nz + z] = value
        if r < REACH - 1:
            own_ref[(REACH - 1) * nz + r] = tile
        strip_ref[r] = strip_of(tiles)

    def x_at(r, d=0):
        return [xs[d, r, z] for z in range(nz)]

    def around(ref, r):
        return lambda j, q: [[ref[j, q, r + d, z] for z in range(nz)] for d in (-1, 0, 1)]

    for r in range(local):
        first_step(coefs(r), x_at(r), ub, r, nz)

    def second(r, carry):
        def store(j, q, z, value):
            vb[j, q, r, z] = value

        second_step(coefs(r), x_at(r), x_at(r, 1), x_at(r, 2), around(ub, r), store, nz)
        return carry

    lax.fori_loop(1, local - 1, second, 0)
    for j in range(POINTS):
        for q in range(2):
            for r in range(1, REACH):
                for z in range(nz):
                    edge_ref[j, q, r - 1, z] = vb[j, q, r, z]

    def third(r, carry):
        for z, value in enumerate(third_step(coefs(r), x_at(r), around(vb, r), nz)):
            part_ref[r - 2, z] = value
        return carry

    lax.fori_loop(2, local - 2, third, 0)


def strip_kernel(recv_ref, strip_ref, pot_strip_ref, all_ref, pot_ref, send_ref):
    nz = recv_ref.shape[0] // REACH - 1
    local = strip_ref.shape[0]
    total = local + REACH
    pairs = total // 2
    sub = sub_ids()
    outer = outer_lanes()
    pots = [jnp.zeros((SUB, LANES), jnp.float32) for _ in range(pot_ref.shape[0])]
    sends = []
    for ri in range(total):
        if ri < REACH:
            k = REACH - 1 - ri
            strip = strip_of([recv_ref[k * nz + z] for z in range(nz)])
            pot = strip_of_layers(recv_ref[REACH * nz + k])
        else:
            strip = strip_ref[ri - REACH]
            pot = pot_strip_ref[ri - REACH]
        all_ref[ri] = strip
        sends.append(send_strip(strip))
        pots[ri // SUB] = jnp.where(sub == ri % SUB, pot, pots[ri // SUB])
    for ri in range(pairs):
        send_ref[ri] = jnp.where(outer, sends[ri], turn(sends[ri + pairs], 8))
    for t, value in enumerate(pots):
        pot_ref[t] = value
        send_ref[pairs + t] = send_strip(value)


def gram_sums(other_of, value, image, grams, images):
    for s in range(len(grams)):
        other = other_of if s == 0 else pltpu.roll(other_of, SUB - s, 0)
        grams[s] = add(grams[s], other * value)
        images[s] = add(images[s], other * image)


def border_kernel(
    own_ref, recv_ref, edge_ref, part_ref, pot_ref, out_ref, sums_ref, tab, xs, ub, vb
):
    cp = lax.axis_index("cp")
    nz, rows, _ = pot_ref.shape
    half = rows // 2
    span = REACH + 2
    table = tab.reshape((POINTS * TABLES + 1) * span * nz, LANES)

    def coefs(r):
        def coef(j, q, z):
            return spread(table, ((j * TABLES + q) * span + r + REACH) * nz + z)

        return coef

    def x_at(r):
        return [own_ref[r * nz + z] if r >= 0 else recv_ref[(-1 - r) * nz + z] for z in range(nz)]

    def around(ref, r):
        def one(j, q, row):
            if row >= 1 and ref is vb:
                return [edge_ref[j, q, row - 1, z] for z in range(nz)]
            return [ref[j, q, row + REACH, z] for z in range(nz)]

        return lambda j, q: [one(j, q, r + d) for d in (-1, 0, 1)]

    for r in range(-REACH, 2):
        tile = own_ref[(REACH - 1) * nz + r] if r >= 0 else recv_ref[REACH * nz - 1 - r]
        fill_tables(tab, tile, lambda index: index * span + r + REACH, min(r + REACH, 2) + 1)
    for r in range(-REACH, 2):
        first_step(coefs(r), x_at(r), ub, r + REACH, nz)
    for r in range(1 - REACH, 1):
        def store(j, q, z, value):
            vb[j, q, r + REACH, z] = value

        x = x_at(r)
        left = [turn(value, 1) for value in x]
        right = [turn(value, -1) for value in x]
        second_step(coefs(r), x, left, right, around(ub, r), store, nz)
    for r in range(-1, 2):
        for z, value in enumerate(third_step(coefs(r), x_at(r), around(vb, r), nz)):
            out_ref[r + 1, z] = value

    lane = lane_ids()
    kept = (lane >= EDGE) & (lane < LANES - EDGE)
    pot = pot_ref.reshape(nz * rows, LANES)
    count = SUB // 2 + 1
    grams, images = [None] * count, [None] * count

    def row_of(r):
        return [out_ref[r + 1, z] if r < 2 else part_ref[r - 2, z] for z in range(nz)]

    for r in range(half):
        row = r + cp * (rows - 1 - 2 * r)
        above, below = row_of(r - 1), row_of(r + 1)
        here = [jnp.where(kept, value, 0.0) for value in row_of(r)]
        for z in range(nz):
            value = here[z]
            near = cross((above, here, below), z) + (turn(value, 1) + turn(value, -1))
            image = (diag_shift + spread(pot, z * rows + row)) * value - kinetic_half * near
            gram_sums(value, value, image, grams, images)
    for s, value in enumerate(grams + images):
        sums_ref[s] = value


def close_kernel(
    all_ref, pot_strip_ref, recv_ref, border_ref, part_ref, sums_ref,
    own_ref, packet_ref, tab, xb, ub, vb, fb,
):
    cp = lax.axis_index("cp")
    nz, half = own_ref.shape[:2]
    total = all_ref.shape[0]
    pairs = total // 2
    tiles = pot_strip_ref.shape[0]
    lane = lane_ids()
    col = column_ids()
    outer = outer_lanes()
    lower = lane >= GROUP
    upper = lane < (nz - 1) * GROUP
    shifts = (0, 1, -1, GROUP, -GROUP)
    span = tiles * SUB

    for t in range(tiles):
        value = jnp.where(outer, recv_ref[pairs + t], pot_strip_ref[t])
        pot_strip = value
        tab[POINTS * 20 * tiles + t] = pot_strip
        for d, shift in enumerate(shifts):
            side = value if d == 0 else turn(value, shift)
            for j in range(POINTS):
                for q, item in enumerate(coefficients(side, j)):
                    tab[(j * 20 + d * 4 + q) * tiles + t] = item
    table = tab.reshape((POINTS * 20 + 1) * span, LANES)

    def coef(j, d, q, ri):
        return spread(table, (j * 20 + d * 4 + q) * span + ri)

    for ri in range(total):
        came = recv_ref[ri] if ri < pairs else turn(recv_ref[ri - pairs], -8)
        value = jnp.where(outer, came, all_ref[ri])
        xb[0, ri] = value
        if 1 <= ri < total - 1:
            xb[1, ri] = turn(value, 1)
            xb[2, ri] = turn(value, -1)
            xb[3, ri] = jnp.where(lower, turn(value, GROUP), 0.0)
            xb[4, ri] = jnp.where(upper, turn(value, -GROUP), 0.0)
        for j in range(POINTS):
            for q in range(2):
                ub[j, q, ri] = coef(j, 0, q, ri) * value

    for ri in range(1, total - 1):
        sides = [xb[d, ri] for d in range(5)]
        for j in range(POINTS):
            near = []
            for q in range(2):
                value = ub[j, q, ri - 1] + ub[j, q, ri + 1]
                for d in range(1, 5):
                    value = value + coef(j, d, q, ri) * sides[d]
                near.append(value)
            rest = sides[0] - near[0]
            real, imag = coef(j, 0, 0, ri), coef(j, 0, 1, ri)
            vb[j, 0, ri] = real * rest + imag * near[1]
            vb[j, 1, ri] = imag * rest - real * near[1]

    for ri in range(2, total - 2):
        parts = [None] * 5
        weight = None
        for j in range(POINTS):
            weight = add(weight, coef(j, 0, 2, ri))
            for d in range(5):
                if d == 0:
                    real, imag = [vb[j, q, ri - 1] + vb[j, q, ri + 1] for q in range(2)]
                else:
                    real, imag = vb[j, 0, ri], vb[j, 1, ri]
                parts[d] = add(parts[d], coef(j, d, 3, ri) * imag - coef(j, d, 2, ri) * real)
        value = weight * xb[0, ri] + parts[0]
        value = value + (turn(parts[1], -1) + turn(parts[2], 1))
        value = value + jnp.where(upper, turn(parts[3], -GROUP), 0.0)
        fb[ri] = value + jnp.where(lower, turn(parts[4], GROUP), 0.0)

    count = SUB // 2 + 1
    grams = [sums_ref[s] for s in range(count)]
    images = [sums_ref[count + s] for s in range(count)]
    whole = ((col >= REACH) & (col < REACH + EDGE)) | (
        (col >= GROUP - REACH - EDGE) & (col < GROUP - REACH)
    )
    edge = (lane < EDGE) | (lane >= LANES - EDGE)
    joined = (col >= GROUP - REACH) & (col < GROUP - REACH + EDGE)
    for r in range(half):
        ri = r + REACH
        value = fb[ri]
        left, right = turn(value, 1), turn(value, -1)
        near = (fb[ri - 1] + fb[ri + 1]) + (left + right)
        near = near + jnp.where(lower, turn(value, GROUP), 0.0)
        near = near + jnp.where(upper, turn(value, -GROUP), 0.0)
        pot = spread(table, POINTS * 20 * span + ri)
        image = (diag_shift + pot) * value - kinetic_half * near
        rest = jnp.where(
            col == REACH + EDGE, left, jnp.where(col == GROUP - REACH - EDGE - 1, right, 0.0)
        )
        image = jnp.where(whole, image, -kinetic_half * rest)
        gram_sums(value, jnp.where(whole, value, 0.0), image, grams, images)
        compact = jnp.where(joined, turn(value, 10), value)
        place = r + cp * (half - 1 - 2 * r)
        for z in range(nz):
            base = border_ref[r + 1, z] if r < 2 else part_ref[r - 2, z]
            moved = turn(compact, -EDGE - GROUP * z - (GROUP - REACH - EDGE))
            own_ref[z, place] = jnp.where(edge, moved, base)

    tile = jnp.zeros((SUB, LANES), jnp.float32)
    for s in range(count):
        tile = jnp.where(lane == s, jnp.sum(grams[s], axis=1, keepdims=True), tile)
        tile = jnp.where(lane == SUB + s, jnp.sum(images[s], axis=1, keepdims=True), tile)
    spun = pltpu.roll(tile, 0, 1, stride=GROUP, stride_axis=0)
    line = jnp.sum(spun, axis=0, keepdims=True)
    packet_ref[...] = jnp.broadcast_to(line[None], packet_ref.shape)


def factor_inverse(entry, size):
    work = [[entry(i, k) for k in range(i + 1)] for i in range(size)]
    root = []
    for k in range(size):
        root.append(lax.rsqrt(work[k][k]))
        for i in range(k + 1, size):
            work[i][k] = work[i][k] * root[k]
        for i in range(k + 1, size):
            for m in range(k + 1, i + 1):
                work[i][m] = work[i][m] - work[i][k] * work[m][k]
    inverse = [[None] * (i + 1) for i in range(size)]
    for i in range(size):
        inverse[i][i] = root[i]
        for k in range(i):
            total = None
            for m in range(k, i):
                total = add(total, work[i][m] * inverse[m][k])
            inverse[i][k] = -(total * root[i])
    return inverse


def finish_kernel(
    packet_ref, own_ref, other_ref, basis_hbm, projected_hbm, buf, out, small, sems, *, cells
):
    cp = lax.axis_index("cp")
    nz, half = own_ref.shape[:2]
    vectors = basis_hbm.shape[0]
    for z in range(nz):
        for r in range(half):
            buf[z, cp * half + r] = own_ref[z, r]
            buf[z, (1 - cp) * half + r] = other_ref[z, r]
    lane = lane_ids()
    sub = sub_ids()
    line = packet_ref[0:SUB, :]
    for start in range(SUB, packet_ref.shape[0], SUB):
        line = line + packet_ref[start : start + SUB, :]
    line = all_sublanes(line) * (1.0 / cells)

    def entry(i, k):
        s = (i - k) % SUB
        at = GROUP * k + s if s <= SUB // 2 else GROUP * i + SUB - s
        return jnp.broadcast_to(line[:, at : at + 1], (SUB, LANES))

    inverse = factor_inverse(entry, vectors)
    flat = buf.reshape(nz * 2 * half * vectors, LANES)
    copies = []
    for z in range(nz):
        for block in range(2 * half // SUB):
            loads = [
                flat[pl.ds((z * 2 * half + block * SUB) * vectors + b, SUB, stride=vectors), :]
                for b in range(vectors)
            ]
            for a in range(vectors):
                value = None
                for b in range(a + 1):
                    value = add(value, inverse[a][b] * loads[b])
                out[a, z, block * SUB : (block + 1) * SUB, :] = value
        copies.append(pltpu.make_async_copy(out.at[:, z], basis_hbm.at[:, z], sems.at[z]))
        copies[-1].start()

    tile = jnp.where((lane >> 4) == sub, line, 0.0)
    for shift in (4 * GROUP, 2 * GROUP, GROUP):
        tile = tile + turn(tile, shift)
    tile = turn(tile, -SUB)
    for s in range(SUB // 2 + 1, SUB):
        moved = turn(pltpu.roll(tile, SUB - s, 0), 2 * s - SUB)
        tile = jnp.where(lane == s, moved, tile)
    tile = jnp.where(lane < SUB, tile, 0.0)
    tile = tile + turn(tile, -SUB)
    image = jnp.where(lane < SUB, pltpu.roll(tile, 0, 1, stride=1, stride_axis=0), 0.0)
    whole = jnp.zeros((SUB, LANES), jnp.float32)
    mixed = None
    for b in range(vectors):
        column = jnp.zeros((SUB, LANES), jnp.float32)
        for a in range(b, vectors):
            column = jnp.where(sub == a, inverse[a][b], column)
        whole = jnp.where(lane == b, column, whole)
        mixed = add(mixed, column * image[b : b + 1, :])
    result = jnp.zeros((SUB, LANES), jnp.float32)
    for c in range(vectors):
        part = jnp.sum(mixed * whole[c : c + 1, :], axis=1, keepdims=True)
        result = jnp.where(lane == c, part, result)
    small[...] = result[:, :vectors]
    copies.append(pltpu.make_async_copy(small, projected_hbm, sems.at[nz]))
    copies[-1].start()
    for copy in copies:
        copy.wait()


def call(
    kernel, operands, outs, scratch, spaces, flops=0, out_spaces=None, grant=GRANT, **options
):
    return pl.pallas_call(
        functools.partial(kernel, **options),
        out_shape=[jax.ShapeDtypeStruct(shape, jnp.float32) for shape in outs],
        in_specs=[pl.BlockSpec(memory_space=space) for space in spaces],
        out_specs=[
            pl.BlockSpec(memory_space=space) for space in out_spaces or [pltpu.VMEM] * len(outs)
        ],
        scratch_shapes=scratch,
        compiler_params=pltpu.CompilerParams(vmem_limit_bytes=grant),
        cost_estimate=pl.CostEstimate(
            flops=flops,
            bytes_accessed=sum(value.size * 4 for value in operands)
            + sum(4 * math.prod(shape) for shape in outs),
            transcendentals=0,
        ),
    )(*operands)


def per_device(start_vectors, potential):
    vectors, nz, rows, columns = start_vectors.shape
    half = rows // 2
    local = half + REACH
    total = local + REACH
    height = -(-local // SUB) * SUB
    assert vectors == SUB and nz == SUB and columns == LANES
    assert lax.axis_size("cp") == 2 and rows % SUB == 0 and total % 2 == 0
    vmem, far, hbm = pltpu.VMEM, pl.ANY, pltpu.HBM
    tile = (SUB, LANES)

    def room(*shape):
        return pltpu.VMEM(shape + tile, jnp.float32)

    count = lax.axis_size("gy")
    rings = []
    for g in range(count):
        rings.append((2 * g, 2 * ((g + 1) % count)))
        rings.append((2 * g + 1, 2 * ((g - 1) % count) + 1))
    (rows_out,) = call(
        pack_kernel,
        [pltpu.with_memory_space_constraint(value, hbm) for value in (start_vectors, potential)],
        [(REACH * (nz + 1),) + tile],
        [room(nz, vectors), room(nz), pltpu.SemaphoreType.DMA((vectors + 1,))],
        (hbm, hbm),
    )
    far_rows = lax.ppermute(rows_out, ("gy", "cp"), rings)
    tables = POINTS * TABLES + 1
    part, edge, strip, pot_strip, own_rows = call(
        interior_kernel, (start_vectors, potential),
        [(local - 4, nz) + tile, (POINTS, 2, REACH - 1, nz) + tile]
        + [(local,) + tile] * 2 + [((REACH - 1) * (nz + 1),) + tile],
        [
            pltpu.VMEM((nz, vectors, height, LANES), jnp.float32),
            room(3, local + 2, nz),
            room(tables * (local + 2)),
            room(POINTS, 2, local + 2, nz),
            room(POINTS, 2, local, nz),
            pltpu.SemaphoreType.DMA((vectors,)),
        ],
        (far, vmem), flops=10**8,
    )
    tiles = -(-total // SUB)
    strips, pot_strips, send = call(
        strip_kernel, (far_rows, strip, pot_strip),
        [(total,) + tile, (tiles,) + tile, (total // 2 + tiles,) + tile],
        [], (vmem,) * 3,
    )
    size = lax.axis_size("gx")
    ahead = [(i, (i + 1) % size) for i in range(size)]
    back = [(i, (i - 1) % size) for i in range(size)]
    recv = lax.ppermute(send, "gx", ahead)
    if size > 2:
        other = lax.ppermute(send, "gx", back)
        recv = jnp.where((jnp.arange(LANES) % 8) < 4, recv, other)
    sums = 2 * (SUB // 2 + 1)
    border, partial = call(
        border_kernel, (own_rows, far_rows, edge, part, potential),
        [(REACH, nz) + tile, (sums,) + tile],
        [
            room(tables * (REACH + 2)),
            room(1),
            room(POINTS, 2, REACH + 2, nz),
            room(POINTS, 2, REACH + 2, nz),
        ],
        (vmem,) * 5, flops=3 * 10**7,
    )
    axes = ("gx", "gy", "cp")
    devices = math.prod(lax.axis_size(axis) for axis in axes)
    own, packet = call(
        close_kernel, (strips, pot_strips, recv, border, part, partial),
        [(nz, half) + tile, (devices, 1, LANES)],
        [
            room((POINTS * 20 + 1) * tiles),
            room(5, total),
            room(POINTS, 2, total),
            room(POINTS, 2, total),
            room(total),
        ],
        (vmem,) * 6, flops=10**7,
    )
    other = lax.ppermute(own, "cp", [(0, 1), (1, 0)])
    packets = lax.all_to_all(packet, axes, 0, 0, tiled=True).reshape(devices, LANES)
    cells = float(nz * rows * columns * lax.axis_size("gx") * lax.axis_size("gy"))
    basis, projected = call(
        finish_kernel, (packets, own, other),
        [(vectors, nz, rows, columns), (vectors, vectors)],
        [
            room(nz, rows),
            pltpu.VMEM((vectors, nz, rows, columns), jnp.float32),
            pltpu.VMEM((vectors, vectors), jnp.float32),
            pltpu.SemaphoreType.DMA((nz + 1,)),
        ],
        (vmem, vmem, vmem), out_spaces=(hbm, hbm), cells=cells,
    )
    return (basis, projected)


def solution(mesh):
    in_specs = (P(None, None, "gy", "gx"), P(None, "gy", "gx"))
    out_specs = (P(None, None, "gy", "gx"), P())
    return jax.shard_map(
        per_device, mesh=mesh, in_specs=in_specs, out_specs=out_specs, check_vma=False
    )
```
